512 devices in a mesh: ep: 32 (over z_lo, x), blk: 16 (over y, z_hi, core).
Axes of the slice: x: 4, y: 4, z: 16 (z_hi: 2, z_lo: 8; z = z_hi * 8 + z_lo), core: 2. Of those that a mesh axis runs over, the one named last changes fastest.
Arguments:
- tokens: bfloat16 [65536, 1536], P(('ep', 'blk')), may hold values from -6 to 6
- norm_gain: bfloat16 [1536], replicated, may hold values from 0.099609375 to 1.8984375
- router_weight: bfloat16 [1536, 32], replicated, may hold values from -0.15625 to 0.15625
- routes: int32 [65536, 4], P(('ep', 'blk')), may hold values from 0 to 31, all different within a row; in each aligned block of 128 rows (0 to 127, 128 to 255, ...) at most 24 rows name the same one
- placement: int32 [32], replicated, may hold values from 0 to 31, each once
- gate_weight: bfloat16 [32, 1536, 768], P('ep', 'blk'), may hold values from -0.15625 to 0.15625
- up_weight: bfloat16 [32, 1536, 768], P('ep', 'blk'), may hold values from -0.15625 to 0.15625
- down_weight: bfloat16 [32, 768, 1536], P('ep', 'blk'), may hold values from -0.21875 to 0.21875
Outputs:
- mixed: bfloat16 [65536, 1536], P(('ep', 'blk'))
The draws below stay inside these ranges and needn't reach their ends.
Inputs may be any that keep to these rules, and one draw needn't show every extreme that they name: `routes`: among the rows of one device, each expert is named by at most 24 rows, a bound that some block reaches; a row names 4 different experts. `placement`: each index of ep holds exactly one expert.
All inputs are finite; a program needn't handle non-finite values.
Results may differ from the reference program's by a relative error of at most 0.0071.
Values may be sent and summed in bfloat16 or wider, within the bound.
A program may use at most 64 MiB of HBM per device.

```python
import math
import jax
import jax.numpy as jnp
import numpy as np
from jax import lax

D = 1536
FF = 768
TOPK = 4
TOK_DEV = 128
EXPERTS = 32
CAP = 24
TOKENS = 65536


def level_of(own_key, shape, shards, smallest, top_value):
    def one(axis_at, shards_of):
        heights = jax.random.uniform(jax.random.fold_in(jax.random.fold_in(own_key, 6), axis_at), (shards_of,), jnp.float32, smallest / len(shards), top_value / len(shards))
        return jnp.repeat(jnp.exp(heights), shape[axis_at] // shards_of).reshape((-1,) + (1,) * (len(shape) - axis_at - 1))

    loudness = one(*shards[0])
    for cut in shards[1:]:
        loudness = loudness * one(*cut)
    return loudness


def assign_block(own_key, own, number, rows, number_of, top, most, slope):
    ranking = jax.random.permutation(own_key, number_of)
    heavy_load, ordinary = shares(number_of, rows * top, most, slope, True), shares(number_of, rows * top, most, slope, False)
    places = jnp.arange(number_of)

    def named(sizes, rotation):
        used = int((sizes > 0).sum())
        fixed = max(1, used // 4)
        moved = fixed + (places - fixed + rotation * (used - fixed)) % max(1, number_of - fixed)
        return jnp.zeros((number_of,), jnp.int32).at[ranking[jnp.where(places < fixed, places, moved)]].set(jnp.asarray(sizes, jnp.int32))

    sizes = jnp.where(number % 4 == 0, named(heavy_load, number // 4), named(ordinary, number - number // 4 - 1))
    mixed = jax.random.permutation(jax.random.fold_in(own, 3), number_of)
    giver, receiver = mixed[0:number_of // 2 * 2:2], mixed[1:number_of // 2 * 2:2]
    slack = jnp.minimum(sizes[giver] - 1, most - sizes[receiver]) // 2
    slack = jnp.where((giver == ranking[0]) | (receiver == ranking[0]) | (sizes[receiver] == 0), 0, jnp.maximum(slack, 0))
    moved = jax.random.randint(jax.random.fold_in(own, 4), (number_of // 2,), 0, 1 << 20) % (slack + 1)
    sizes = sizes.at[giver].add(-moved).at[receiver].add(moved)
    items = jnp.searchsorted(jnp.cumsum(sizes), jnp.arange(rows * top), side="right").astype(jnp.int32)
    table = items.reshape(top, rows).T
    table = table[jax.random.permutation(jax.random.fold_in(own, 1), rows)]
    rotation = jax.random.randint(jax.random.fold_in(own, 2), (rows, 1), 0, top)
    return jnp.take_along_axis(table, (jnp.arange(top)[None, :] + rotation) % top, axis=1)


def shares(amount, total, bound, slope, full):
    portions = [(1 << 20) // math.isqrt(standing ** slope) + 1 for standing in range(1, amount + 1)]
    largest = bound if full else min(bound, max(-(-total // amount), total * portions[0] // sum(portions)))
    least = 1 if total - largest >= amount - 1 else 0
    holding, spare = [largest] + [least] * (amount - 1), total - largest - least * (amount - 1)
    while spare > 0:
        candidates = [i for i in range(1, amount) if holding[i] < largest] or [i for i in range(1, amount) if holding[i] < bound]
        pool, remaining = sum([portions[i] for i in candidates]), spare
        for i in candidates:
            more = min(bound - holding[i], max(1, remaining * portions[i] // pool), spare)
            holding[i] = holding[i] + more
            spare = spare - more
    return np.array(holding)


def gaussian(rng, dims, spread, most, cuts=(), kind=jnp.bfloat16):
    gain = level_of(rng, dims, cuts, -0.22, 0.18) if cuts else 1.0
    array = jax.random.normal(rng, dims, jnp.float32) * spread * gain
    return jnp.minimum(jnp.maximum(array, -most), most).astype(kind)


def setup_inputs(seed: int = 0) -> dict:
    streams_of = jax.random.split(jax.random.key(seed), 9)
    tokens = gaussian(streams_of[0], (TOKENS, D), 1.0, 6.0, ((0, 512),))
    norm_gain = jnp.clip(1.0 + 0.18 * jax.random.normal(streams_of[1], (D,), jnp.float32), 0.099609375, 1.8984375).astype(jnp.bfloat16)
    router_weight = gaussian(streams_of[2], (D, EXPERTS), D ** -0.5, 0.15625)
    routes_keys = jax.random.split(jax.random.fold_in(streams_of[3], 1), TOKENS // TOK_DEV)
    routes_turns = jax.random.permutation(jax.random.fold_in(streams_of[3], 3), TOKENS // TOK_DEV)
    routes = jax.vmap(lambda own, number: assign_block(jax.random.fold_in(streams_of[3], 2), own, number, TOK_DEV, EXPERTS, TOPK, CAP, 2))(routes_keys, routes_turns).reshape((TOKENS, TOPK))
    placement = jax.random.permutation(streams_of[4], EXPERTS).astype(jnp.int32)
    gate_weight = gaussian(streams_of[5], (EXPERTS, D, FF), D ** -0.5, 0.15625, ((0, 32), (1, 16)))
    up_weight = gaussian(streams_of[6], (EXPERTS, D, FF), D ** -0.5, 0.15625, ((0, 32), (1, 16)))
    down_weight = gaussian(streams_of[7], (EXPERTS, FF, D), FF ** -0.5, 0.21875, ((0, 32), (1, 16)))
    return {"tokens": tokens, "norm_gain": norm_gain, "router_weight": router_weight, "routes": routes, "placement": placement, "gate_weight": gate_weight, "up_weight": up_weight, "down_weight": down_weight}


def reference(tokens, norm_gain, router_weight, routes, placement, gate_weight, up_weight, down_weight):
    values = tokens.astype(jnp.float32)
    square = lax.optimization_barrier(jnp.mean(values * values, axis=-1, keepdims=True))
    normed = (values * lax.rsqrt(square + 1e-06) * norm_gain.astype(jnp.float32)).astype(jnp.bfloat16)
    logits = jnp.dot(normed, router_weight, preferred_element_type=jnp.float32)
    picked = jax.nn.sigmoid(jnp.take_along_axis(logits, routes, axis=1))
    gates = picked / lax.optimization_barrier(jnp.sum(picked, axis=1, keepdims=True))
    blocks = TOKENS // TOK_DEV
    assigned = TOK_DEV * TOPK
    flat_ids = routes.reshape(blocks, assigned)
    onehot = (flat_ids[:, :, None] == jnp.arange(EXPERTS, dtype=jnp.int32)[None, None, :]).astype(jnp.int32)
    counts = jnp.cumsum(onehot, axis=1)
    slots = lax.optimization_barrier(jnp.sum(onehot * (counts - 1), axis=-1)).astype(jnp.int32)
    targets = (jnp.arange(blocks, dtype=jnp.int32)[:, None] * CAP + slots).reshape(-1)
    flat_ids = flat_ids.reshape(-1)
    flat_gates = gates.reshape(-1)
    total = blocks * CAP
    everyone = jnp.arange(TOKENS * TOPK, dtype=jnp.int32)

    def expert_step(acc, expert):
        match = flat_ids == expert
        where_to = jnp.where(match, targets, total).astype(jnp.int32)
        owner = jnp.full((total,), -1, jnp.int32).at[where_to].set(everyone, mode='drop')
        valid = owner >= 0
        owned = jnp.maximum(owner, 0)
        token_rows = owned // TOPK
        buffer = jnp.where(valid[:, None], normed[token_rows], jnp.zeros((), jnp.bfloat16))
        holder = placement[expert]
        gate = jnp.dot(buffer, gate_weight[holder], preferred_element_type=jnp.float32)
        upper = jnp.dot(buffer, up_weight[holder], preferred_element_type=jnp.float32)
        hidden = (jax.nn.relu(gate) * upper).astype(jnp.bfloat16)
        rows_out = jnp.dot(hidden, down_weight[holder], preferred_element_type=jnp.float32).astype(jnp.bfloat16)
        weights = jnp.where(valid, flat_gates[owned], jnp.zeros((), jnp.float32))
        acc = acc.at[token_rows].add(weights[:, None] * rows_out.astype(jnp.float32))
        return (acc, None)
    start = jnp.zeros((TOKENS, D), jnp.float32)
    acc, unused = lax.scan(expert_step, start, jnp.arange(EXPERTS, dtype=jnp.int32))
    return acc.astype(jnp.bfloat16)
```

```python
import functools

import jax
import jax.numpy as jnp
from jax import lax
from jax.experimental import pallas as pl
from jax.experimental.pallas import tpu as pltpu
from jax.sharding import PartitionSpec as P

MESH = pl.DeviceIdType.MESH
NZ, NX, NY = 8, 4, 4
CAP = 24
LAG_EXPERT = 4
LAG_MIX = 5
LAG_SUM = 6
STEPS = NZ - 1 + LAG_SUM
WEIGHTS_AT = 5
AG_PIECES = 2
RS_PIECES = 4


def kernel(
    tokens, gain, routes_t, router_t, placement, gate_w, up_w, down_w, out,
    tok, met, wgu, wdn, rel_gu, rel_dn, xs, xr, ys, yr, hid, part, rin_b, rin_f, rout,
    loc_sem, z_s, z_r, yo_s, yo_r, yp_s, yp_r, y2_s, y2_r, c_s, c_r,
    ag_s, ag_r, mg_s, mg_r, xd_s, xd_r, xb_s, xb_r, rs_s, rs_rb, rs_rf,
):
    f32, bf16 = jnp.float32, jnp.bfloat16
    ep, blk = lax.axis_index("ep"), lax.axis_index("blk")
    z, x = ep // NX, ep % NX
    y, zh, c = blk // 4, (blk // 2) % 2, blk % 2
    width = tokens.shape[1]
    rows = tokens.shape[0]
    grows, drows = gate_w.shape[0], down_w.shape[0]
    ff = gate_w.shape[1]

    def blk_of(yy, zz, cc):
        return ((yy + NY) % NY) * 4 + zz * 2 + cc

    def at_z(zz):
        return {"ep": zz * NX + x, "blk": blk}

    def at_x(xx):
        return {"ep": z * NX + xx, "blk": blk}

    up4 = {"ep": ((z + 4) % NZ) * NX + x, "blk": blk_of(y, (zh + z // 4) % 2, c)}
    dn4_zh = (zh + 1 - z // 4) % 2
    dn4 = {"ep": ((z + 4) % NZ) * NX + x, "blk": blk_of(y, dn4_zh, c)}
    up4_zh = (zh + z // 4) % 2
    y_up = {"ep": ep, "blk": blk_of(y + 1, zh, c)}
    y_dn = {"ep": ep, "blk": blk_of(y - 1, zh, c)}
    core = {"ep": ep, "blk": blk_of(y, zh, 1 - c)}

    def remote(src, dst, s, r, dev):
        return pltpu.make_async_remote_copy(
            src_ref=src, dst_ref=dst, send_sem=s, recv_sem=r, device_id=dev, device_id_type=MESH
        )

    def gu_at(b):
        return wgu.at[pl.ds(pl.multiple_of(b * grows, grows), grows)]

    def dn_at(b):
        return wdn.at[pl.ds(pl.multiple_of(b * drows, drows), drows)]

    own = pl.ds(pl.multiple_of(blk * grows, grows), grows)
    local = [
        pltpu.make_async_copy(gate_w, wgu.at[own, pl.ds(0, ff)], loc_sem.at[0]),
        pltpu.make_async_copy(up_w, wgu.at[own, pl.ds(ff, ff)], loc_sem.at[1]),
        pltpu.make_async_copy(down_w, dn_at(blk), loc_sem.at[2]),
    ]
    for copy in local:
        copy.start()

    barrier = pltpu.get_barrier_semaphore()

    def greet(dev):
        pl.semaphore_signal(barrier, inc=1, device_id=dev, device_id_type=MESH)

    for dev in (up4, dn4, y_up, y_dn, core):
        greet(dev)
    for j in range(1, NX):
        greet(at_x((x + j) % NX))

    @pl.when(z > 0)
    def _():
        greet(at_z(z - 1))

    @pl.when(z < NZ - 1)
    def _():
        greet(at_z(z + 1))

    peers = 8 + (z > 0).astype(jnp.int32) + (z < NZ - 1).astype(jnp.int32)
    pl.semaphore_wait(barrier, peers)

    for copy in local:
        copy.wait()

    half_g, half_d = grows // 2, width // 2

    def gu_half(b, h):
        return wgu.at[pl.ds(pl.multiple_of(b * grows + h * half_g, half_g), half_g)]

    def dn_half(b, h):
        return wdn.at[pl.ds(pl.multiple_of(b * drows, drows), drows), pl.ds(h * half_d, half_d)]

    hop1, hop2 = [], []
    for h, dev, owner in ((0, up4, blk_of(y, dn4_zh, c)), (1, dn4, blk_of(y, up4_zh, c))):
        hop1 += [
            remote(gu_half(blk, h), rel_gu.at[h], z_s.at[0, h, 0], z_r.at[0, h, 0], dev),
            remote(dn_half(blk, h), rel_dn.at[h], z_s.at[0, h, 1], z_r.at[0, h, 1], dev),
        ]
        hop2 += [
            remote(rel_gu.at[h], gu_half(owner, h), z_s.at[1, h, 0], z_r.at[1, h, 0], dev),
            remote(rel_dn.at[h], dn_half(owner, h), z_s.at[1, h, 1], z_r.at[1, h, 1], dev),
        ]
    mate = blk_of(y, 1 - zh, c)

    def shard_to(b, s, r, dev):
        return [
            remote(gu_at(b), gu_at(b), s.at[0], r.at[0], dev),
            remote(dn_at(b), dn_at(b), s.at[1], r.at[1], dev),
        ]

    def start(copies):
        for copy in copies:
            copy.start()

    def wait_recv(copies):
        for copy in copies:
            copy.wait_recv()

    def wait_send(copies):
        for copy in copies:
            copy.wait_send()

    mine_up = shard_to(blk, yo_s.at[0], yo_r.at[0], y_up)
    mine_dn = shard_to(blk, yo_s.at[1], yo_r.at[1], y_dn)
    from_dn = shard_to(blk_of(y - 1, zh, c), yo_s.at[0], yo_r.at[0], y_dn)
    from_up = shard_to(blk_of(y + 1, zh, c), yo_s.at[1], yo_r.at[1], y_up)
    mate_up = shard_to(mate, yp_s.at[0], yp_r.at[0], y_up)
    mate_dn = shard_to(mate, yp_s.at[1], yp_r.at[1], y_dn)
    mate_from_dn = shard_to(blk_of(y - 1, 1 - zh, c), yp_s.at[0], yp_r.at[0], y_dn)
    mate_from_up = shard_to(blk_of(y + 1, 1 - zh, c), yp_s.at[1], yp_r.at[1], y_up)
    far_own = shard_to(blk_of(y - 1, zh, c), y2_s.at[0], y2_r.at[0], y_up)
    far_mate = shard_to(blk_of(y + 1, 1 - zh, c), y2_s.at[1], y2_r.at[1], y_dn)
    far_own_in = shard_to(blk_of(y - 2, zh, c), y2_s.at[0], y2_r.at[0], y_dn)
    far_mate_in = shard_to(blk_of(y + 2, 1 - zh, c), y2_s.at[1], y2_r.at[1], y_up)
    held = [(0, zh), (-1, zh), (1, zh), (2, zh), (0, 1 - zh), (-1, 1 - zh), (1, 1 - zh), (2, 1 - zh)]
    to_core = [shard_to(blk_of(y + dy, zz, c), c_s.at[k], c_r.at[k], core) for k, (dy, zz) in enumerate(held)]
    of_core = [shard_to(blk_of(y + dy, zz, 1 - c), c_s.at[k], c_r.at[k], core) for k, (dy, zz) in enumerate(held)]

    start(hop1)
    start(mine_up)
    start(mine_dn)
    start(to_core[0])

    values = tokens[...].astype(f32)
    square = jnp.mean(values * values, axis=-1, keepdims=True)
    normed = (values * lax.rsqrt(square + 1e-06) * gain[...].astype(f32)).astype(bf16)
    tok[z] = normed
    experts = router_t.shape[0]
    holder = lax.broadcasted_iota(jnp.int32, (experts, experts), 0)
    placed = (holder == placement[...]).astype(f32).astype(bf16)
    expert_row = lax.broadcasted_iota(jnp.int32, (experts, rows), 0)
    named = jnp.zeros((experts, rows), f32)
    for k in range(routes_t.shape[0]):
        named = named + (expert_row == routes_t[pl.ds(k, 1), :]).astype(f32)
    named = jnp.dot(placed, named.astype(bf16), preferred_element_type=f32)
    earlier = lax.broadcasted_iota(jnp.int32, (rows, rows), 0) < lax.broadcasted_iota(
        jnp.int32, (rows, rows), 1
    )
    before = jnp.dot(named.astype(bf16), earlier.astype(f32).astype(bf16), preferred_element_type=f32)
    slot = jnp.where(named > 0.5, before + 1.0, 0.0)
    router_p = jnp.dot(placed, router_t[...], preferred_element_type=f32).astype(bf16)
    logits = lax.dot_general(
        router_p, normed, (((1,), (1,)), ((), ())), preferred_element_type=f32
    )
    picked = jnp.where(named > 0.5, jax.nn.sigmoid(logits), 0.0)
    gates = picked / jnp.sum(picked, axis=0, keepdims=True)
    for zz in range(NZ):
        met[z, zz, pl.ds(0, NX), :] = slot[zz * NX : (zz + 1) * NX]
        met[z, zz, pl.ds(NX, NX), :] = gates[zz * NX : (zz + 1) * NX]

    piece = rows // AG_PIECES

    def block_to(way, s, d, zz):
        copies = [remote(met.at[s], met.at[s], mg_s.at[way, d], mg_r.at[way, d], at_z(zz))]
        for p in range(AG_PIECES):
            part_of = tok.at[s, pl.ds(p * piece, piece)]
            copies.append(remote(part_of, part_of, ag_s.at[way, d, p], ag_r.at[way, d, p], at_z(zz)))
        return copies

    @pl.when(z < NZ - 1)
    def _():
        start(block_to(0, z, 1, z + 1))

    @pl.when(z > 0)
    def _():
        start(block_to(1, z, 1, z - 1))

    for one, two in zip(hop1, hop2):
        one.wait_recv()
        two.start()
    wait_recv(from_dn)
    start(far_own)
    start(to_core[1])
    wait_recv(from_up)
    start(to_core[2])

    def pair_at(d):
        left = (z + d) % 2 == 0
        q = jnp.where(left, (z - d) // 2, (z + d - 1) // 2)
        valid = jnp.logical_and(d >= 1, jnp.where(left, z - d >= 0, z + d - 1 <= NZ - 1))
        return jnp.where(valid, q, 0), valid

    def spread(q, row):
        pieces = []
        token_block = lax.broadcasted_iota(jnp.int32, (1, 2 * rows), 1) // rows
        for xx in range(NX):
            both = jnp.concatenate(
                [met[2 * q, z, pl.ds(row + xx, 1), :], met[2 * q + 1, z, pl.ds(row + xx, 1), :]], axis=1
            )
            for h in range(2):
                pieces.append(jnp.where(token_block == h, both, 0.0))
        return pieces

    slot_of = lax.broadcasted_iota(jnp.int32, (CAP, 2 * rows), 0).astype(f32) + 1.0
    pair_rows = 2 * CAP

    def gather(q):
        pick = jnp.concatenate([(line == slot_of).astype(f32) for line in spread(q, 0)], axis=0).astype(bf16)

        @pl.loop(0, width // 256)
        def _(n):
            cols = pl.ds(pl.multiple_of(n * 256, 256), 256)
            pair = tok[pl.ds(2 * q, 2), :, cols].reshape(2 * rows, 256)
            got = jnp.dot(pick, pair, preferred_element_type=f32).astype(bf16)
            for xx in range(NX):
                xs[q, xx, :, cols] = got[xx * pair_rows : (xx + 1) * pair_rows]

        for j in range(1, NX):
            to = (x + j) % NX
            remote(xs.at[q, to], xr.at[q, x], xd_s.at[q, j], xd_r.at[q, j], at_x(to)).start()
        xr[q, x] = xs[q, x]

    def expert(q):
        for j in range(1, NX):
            src = (x + NX - j) % NX
            remote(xs.at[q, src], xr.at[q, src], xd_s.at[q, j], xd_r.at[q, j], at_x(src)).wait_recv()
        row_in = xr[q].reshape(NX * pair_rows, width)

        @pl.loop(0, ff // 256)
        def _(n):
            at_gate = pl.ds(pl.multiple_of(n * 256, 256), 256)
            at_up = pl.ds(pl.multiple_of(ff + n * 256, 256), 256)
            gate = jnp.dot(row_in, wgu[:, at_gate], preferred_element_type=f32)
            upper = jnp.dot(row_in, wgu[:, at_up], preferred_element_type=f32)
            hid[:, at_gate] = (jnp.maximum(gate, 0.0) * upper).astype(bf16)

        hidden = hid[...]

        @pl.loop(0, width // 256)
        def _(n):
            cols = pl.ds(pl.multiple_of(n * 256, 256), 256)
            got = jnp.dot(hidden, wdn[:, cols], preferred_element_type=f32).astype(bf16)
            for xx in range(NX):
                ys[q, xx, :, cols] = got[xx * pair_rows : (xx + 1) * pair_rows]

        for j in range(1, NX):
            to = (x + j) % NX
            remote(ys.at[q, to], yr.at[q, x], xb_s.at[q, j], xb_r.at[q, j], at_x(to)).start()
        yr[q, x] = ys[q, x]

    def mix(q):
        for j in range(1, NX):
            src = (x + NX - j) % NX
            remote(ys.at[q, src], yr.at[q, src], xb_s.at[q, j], xb_r.at[q, j], at_x(src)).wait_recv()
        weigh = jnp.concatenate(
            [
                jnp.where(line == slot_of, gate, 0.0)
                for line, gate in zip(spread(q, 0), spread(q, NX))
            ],
            axis=0,
        )
        high = weigh.astype(bf16)
        low = (weigh - high.astype(f32)).astype(bf16)
        high, low = high.T, low.T

        @pl.loop(0, width // 256)
        def _(n):
            cols = pl.ds(pl.multiple_of(n * 256, 256), 256)
            back = yr[q, :, :, cols].reshape(NX * pair_rows, 256)
            total = jnp.dot(high, back, preferred_element_type=f32) + jnp.dot(
                low, back, preferred_element_type=f32
            )
            part[pl.ds(2 * q, 2), :, cols] = total.reshape(2, rows, 256)

    rs_piece = rows // RS_PIECES

    def add_and_send(s, rin, rs_r, first, to):
        for p in range(RS_PIECES):
            at = pl.ds(p * rs_piece, rs_piece)
            copy = remote(rout.at[s, at], rin.at[s, at], rs_s.at[s, p], rs_r.at[s, p], at_z(to))

            @pl.when(first)
            def _():
                rout[s, at] = part[s, at].astype(bf16)

            @pl.when(jnp.logical_not(first))
            def _():
                copy.wait_recv()
                rout[s, at] = (part[s, at] + rin[s, at].astype(f32)).astype(bf16)

            copy.start()

    def step(d, carry):
        @pl.when(jnp.logical_and(d < NZ, z >= d))
        def _():
            got = block_to(0, z - d, d, jnp.minimum(z + 1, NZ - 1))
            send = block_to(0, z - d, d + 1, jnp.minimum(z + 1, NZ - 1))
            for one, two in zip(got, send):
                one.wait_recv()

                @pl.when(z < NZ - 1)
                def _():
                    two.start()

        @pl.when(jnp.logical_and(d < NZ, z + d <= NZ - 1))
        def _():
            got = block_to(1, z + d, d, jnp.maximum(z - 1, 0))
            send = block_to(1, z + d, d + 1, jnp.maximum(z - 1, 0))
            for one, two in zip(got, send):
                one.wait_recv()

                @pl.when(z > 0)
                def _():
                    two.start()

        @pl.when(d == 2)
        def _():
            wait_recv(hop2)
            start(mate_up)
            start(mate_dn)
            start(to_core[4])
            wait_recv(far_own_in)
            start(to_core[3])

        @pl.when(d == 3)
        def _():
            wait_recv(mate_from_up)
            start(far_mate)
            start(to_core[6])
            wait_recv(mate_from_dn)
            start(to_core[5])

        @pl.when(d == 4)
        def _():
            wait_recv(far_mate_in)
            start(to_core[7])

        q, valid = pair_at(d)

        @pl.when(valid)
        def _():
            gather(q)

        @pl.when(d == WEIGHTS_AT)
        def _():
            for copies in of_core:
                wait_recv(copies)

        q_e, valid_e = pair_at(d - LAG_EXPERT)

        @pl.when(valid_e)
        def _():
            expert(q_e)

        q_m, valid_m = pair_at(d - LAG_MIX)

        @pl.when(valid_m)
        def _():
            mix(q_m)

        s_b = NZ - 1 + LAG_SUM - d

        @pl.when(jnp.logical_and(s_b >= 0, s_b < z))
        def _():
            add_and_send(s_b, rin_b, rs_rb, z == NZ - 1, z - 1)

        s_f = d - LAG_SUM

        @pl.when(jnp.logical_and(s_f > z, s_f <= NZ - 1))
        def _():
            add_and_send(s_f, rin_f, rs_rf, z == 0, z + 1)

        return carry

    lax.fori_loop(1, STEPS + 1, step, 0)

    for p in range(RS_PIECES):
        at = pl.ds(p * rs_piece, rs_piece)

        @pl.when(z < NZ - 1)
        def _():
            remote(rout.at[z, at], rin_b.at[z, at], rs_s.at[z, p], rs_rb.at[z, p], at_z(z + 1)).wait_recv()
            part[z, at] = part[z, at] + rin_b[z, at].astype(f32)

        @pl.when(z > 0)
        def _():
            remote(rout.at[z, at], rin_f.at[z, at], rs_s.at[z, p], rs_rf.at[z, p], at_z(z - 1)).wait_recv()
            part[z, at] = part[z, at] + rin_f[z, at].astype(f32)

        out[at, :] = part[z, at].astype(bf16)

    wait_send(hop1 + hop2 + mine_up + mine_dn + mate_up + mate_dn + far_own + far_mate)
    for copies in to_core:
        wait_send(copies)

    def drain(d, carry):
        @pl.when(jnp.logical_and(z < NZ - 1, z >= d - 1))
        def _():
            wait_send(block_to(0, z - d + 1, d, z + 1))

        @pl.when(jnp.logical_and(z > 0, z + d - 1 <= NZ - 1))
        def _():
            wait_send(block_to(1, z + d - 1, d, z - 1))

        return carry

    lax.fori_loop(1, NZ, drain, 0)

    def drain_pair(q, carry):
        for j in range(1, NX):
            to = (x + j) % NX
            remote(xs.at[q, to], xr.at[q, x], xd_s.at[q, j], xd_r.at[q, j], at_x(to)).wait_send()
            remote(ys.at[q, to], yr.at[q, x], xb_s.at[q, j], xb_r.at[q, j], at_x(to)).wait_send()
        return carry

    lax.fori_loop(0, NZ // 2, drain_pair, 0)

    def drain_sum(s, carry):
        @pl.when(s != z)
        def _():
            for p in range(RS_PIECES):
                at = pl.ds(p * rs_piece, rs_piece)
                remote(
                    rout.at[s, at], rin_b.at[s, at], rs_s.at[s, p], rs_rb.at[s, p],
                    at_z(jnp.where(s < z, z - 1, z + 1)),
                ).wait_send()

        return carry

    lax.fori_loop(0, NZ, drain_sum, 0)


def on_device(
    tokens, norm_gain, router_weight, routes, placement, gate_weight, up_weight, down_weight
):
    rows, width = tokens.shape
    experts = router_weight.shape[1]
    ff = gate_weight.shape[2]
    grows, drows = gate_weight.shape[1], down_weight.shape[1]
    blks = lax.axis_size("blk")
    bf16, f32 = jnp.bfloat16, jnp.float32
    dma = pltpu.SemaphoreType.DMA
    vmem = pl.BlockSpec(memory_space=pltpu.VMEM)
    hbm = pl.BlockSpec(memory_space=pl.ANY)
    rows_of = (NZ // 2, NX, 2 * CAP, width)
    return pl.pallas_call(
        kernel,
        out_shape=jax.ShapeDtypeStruct((rows, width), bf16),
        in_specs=[vmem] * 5 + [hbm] * 3,
        out_specs=vmem,
        scratch_shapes=[
            pltpu.VMEM((NZ, rows, width), bf16),
            pltpu.VMEM((NZ, NZ, 2 * NX, rows), f32),
            pltpu.VMEM((blks * grows, 2 * ff), bf16),
            pltpu.VMEM((blks * drows, width), bf16),
            pltpu.VMEM((2, grows // 2, 2 * ff), bf16),
            pltpu.VMEM((2, drows, width // 2), bf16),
            pltpu.VMEM(rows_of, bf16),
            pltpu.VMEM(rows_of, bf16),
            pltpu.VMEM(rows_of, bf16),
            pltpu.VMEM(rows_of, bf16),
            pltpu.VMEM((NX * 2 * CAP, ff), bf16),
            pltpu.VMEM((NZ, rows, width), f32),
            pltpu.VMEM((NZ, rows, width), bf16),
            pltpu.VMEM((NZ, rows, width), bf16),
            pltpu.VMEM((NZ, rows, width), bf16),
            dma((3,)),
            dma((2, 2, 2)), dma((2, 2, 2)),
            dma((2, 2)), dma((2, 2)), dma((2, 2)), dma((2, 2)), dma((2, 2)), dma((2, 2)),
            dma((8, 2)), dma((8, 2)),
            dma((2, NZ + 1, AG_PIECES)), dma((2, NZ + 1, AG_PIECES)),
            dma((2, NZ + 1)), dma((2, NZ + 1)),
            dma((NZ // 2, NX)), dma((NZ // 2, NX)), dma((NZ // 2, NX)), dma((NZ // 2, NX)),
            dma((NZ, RS_PIECES)), dma((NZ, RS_PIECES)), dma((NZ, RS_PIECES)),
        ],
        compiler_params=pltpu.CompilerParams(
            collective_id=0, has_side_effects=True, vmem_limit_bytes=60 * 1024 * 1024
        ),
    )(
        tokens,
        norm_gain.reshape(1, width),
        routes.T,
        router_weight.T,
        placement.reshape(1, experts),
        gate_weight[0],
        up_weight[0],
        down_weight[0],
    )


def solution(mesh):
    in_specs = (
        P(("ep", "blk"), None),
        P(),
        P(),
        P(("ep", "blk"), None),
        P(),
        P("ep", "blk", None),
        P("ep", "blk", None),
        P("ep", "blk", None),
    )
    out_specs = P(("ep", "blk"), None)
    return jax.shard_map(
        on_device, mesh=mesh, in_specs=in_specs, out_specs=out_specs, check_vma=False
    )
```

```python
import functools

import jax
import jax.numpy as jnp
from jax import lax
from jax.experimental import pallas as pl
from jax.experimental.pallas import tpu as pltpu
from jax.sharding import PartitionSpec as P

MESH = pl.DeviceIdType.MESH
NZ, NX, NY = 8, 4, 4
CAP = 24
PIECES = 4
LAG_EXPERT = 6
LAG_MIX = 12
LAG_SUM = 2 * PIECES + LAG_MIX
HOP = 7
TICKS = (NZ - 1) * PIECES + ((NZ - 1) * HOP + 3) // 4 + LAG_SUM + 4
MATE_AT = (2, 5, 9)
OWN_ROWS_AT = 4
MATE_ROWS_AT = (8, 11, 13)
WEIGHTS_AT = 2 * PIECES - 1 + LAG_EXPERT


def kernel(
    tokens, gain, routes_t, router_t, placement, gate_w, up_w, down_w, out,
    tok, met, wgu, wdn, xs, xr, ys, yr, hid, part, rin_b, rin_f, rout,
    loc_sem, z_s, z_r, yo_s, yo_r, yp_s, yp_r, co_s, co_r, cp_s, cp_r,
    ag_s, ag_r, mg_s, mg_r, xd_s, xd_r, xb_s, xb_r, rs_s, rs_rb, rs_rf,
):
    f32, bf16 = jnp.float32, jnp.bfloat16
    ep, blk = lax.axis_index("ep"), lax.axis_index("blk")
    z, x = ep // NX, ep % NX
    y, zh, c = blk // 4, (blk // 2) % 2, blk % 2
    width = tokens.shape[1]
    rows = tokens.shape[0]
    grows, drows = gate_w.shape[0], down_w.shape[0]
    ff = gate_w.shape[1]

    def blk_of(yy, zz, cc):
        return ((yy + NY) % NY) * 4 + zz * 2 + cc

    def at_z(zz):
        return {"ep": zz * NX + x, "blk": blk}

    def at_y(j):
        return {"ep": ep, "blk": blk_of(y + j, zh, c)}

    def at_x(xx):
        return {"ep": z * NX + xx, "blk": blk}

    mate = {"ep": ep, "blk": blk_of(y, 1 - zh, c)}
    core = {"ep": ep, "blk": blk_of(y, zh, 1 - c)}

    def remote(src, dst, s, r, dev):
        return pltpu.make_async_remote_copy(
            src_ref=src, dst_ref=dst, send_sem=s, recv_sem=r, device_id=dev, device_id_type=MESH
        )

    def gu_at(b):
        return wgu.at[pl.ds(pl.multiple_of(b * grows, grows), grows)]

    def dn_at(b):
        return wdn.at[pl.ds(pl.multiple_of(b * drows, drows), drows)]

    own = pl.ds(pl.multiple_of(blk * grows, grows), grows)
    local = [
        pltpu.make_async_copy(gate_w, wgu.at[own, pl.ds(0, ff)], loc_sem.at[0]),
        pltpu.make_async_copy(up_w, wgu.at[own, pl.ds(ff, ff)], loc_sem.at[1]),
        pltpu.make_async_copy(down_w, dn_at(blk), loc_sem.at[2]),
    ]
    for copy in local:
        copy.start()

    barrier = pltpu.get_barrier_semaphore()

    def greet(dev):
        pl.semaphore_signal(barrier, inc=1, device_id=dev, device_id_type=MESH)

    greet(mate)
    greet(core)
    for j in range(1, NY):
        greet(at_y(j))
    for j in range(1, NX):
        greet(at_x((x + j) % NX))

    @pl.when(z > 0)
    def _():
        greet(at_z(z - 1))

    @pl.when(z < NZ - 1)
    def _():
        greet(at_z(z + 1))

    peers = 8 + (z > 0).astype(jnp.int32) + (z < NZ - 1).astype(jnp.int32)
    pl.semaphore_wait(barrier, peers)

    for copy in local:
        copy.wait()

    half_g = grows // 2

    def part_at(b, p):
        if p == 2:
            return dn_at(b)
        return wgu.at[pl.ds(pl.multiple_of(b * grows + p * half_g, half_g), half_g)]

    def part_to(b, p, s, r, dev):
        return remote(part_at(b, p), part_at(b, p), s, r, dev)

    parts = range(3)
    mate_blk = blk_of(y, 1 - zh, c)
    mate_out = [part_to(blk, p, z_s.at[p], z_r.at[p], mate) for p in parts]
    mate_in = [part_to(mate_blk, p, z_s.at[p], z_r.at[p], mate) for p in parts]

    def y_copies(zz, s, r, far):
        return [
            [
                part_to(blk_of(y - j, zz, c) if far else blk_of(y, zz, c), p, s.at[j, p], r.at[j, p], at_y(j))
                for p in parts
            ]
            for j in range(NY)
        ]

    def core_copies(zz, cc, s, r):
        return [
            [part_to(blk_of(y - j, zz, cc), p, s.at[j, p], r.at[j, p], core) for p in parts]
            for j in range(NY)
        ]

    own_out, own_in = y_copies(zh, yo_s, yo_r, False), y_copies(zh, yo_s, yo_r, True)
    pass_out, pass_in = y_copies(1 - zh, yp_s, yp_r, False), y_copies(1 - zh, yp_s, yp_r, True)
    own_core, own_of_core = core_copies(zh, c, co_s, co_r), core_copies(zh, 1 - c, co_s, co_r)
    mate_core, mate_of_core = core_copies(1 - zh, c, cp_s, cp_r), core_copies(1 - zh, 1 - c, cp_s, cp_r)

    for copy in mate_out:
        copy.start()
    for p in parts:
        for j in (1, 3, 2):
            own_out[j][p].start()
        own_core[0][p].start()

    def weights_at(t):
        for p in parts:
            @pl.when(t == MATE_AT[p])
            def _():
                mate_in[p].wait_recv()
                for j in (1, 3, 2):
                    pass_out[j][p].start()
                mate_core[0][p].start()

        @pl.when(t == OWN_ROWS_AT)
        def _():
            for p in parts:
                for j in (1, 3, 2):
                    own_in[j][p].wait_recv()
                    own_core[j][p].start()

        for p in parts:
            @pl.when(t == MATE_ROWS_AT[p])
            def _():
                for j in (1, 3, 2):
                    pass_in[j][p].wait_recv()
                    mate_core[j][p].start()

        @pl.when(t == WEIGHTS_AT)
        def _():
            for copies in own_of_core + mate_of_core:
                for copy in copies:
                    copy.wait_recv()

    values = tokens[...].astype(f32)
    square = jnp.mean(values * values, axis=-1, keepdims=True)
    normed = (values * lax.rsqrt(square + 1e-06) * gain[...].astype(f32)).astype(bf16)
    tok[z] = normed
    experts = router_t.shape[0]
    holder = lax.broadcasted_iota(jnp.int32, (experts, experts), 0)
    placed = (holder == placement[...]).astype(f32).astype(bf16)
    expert_row = lax.broadcasted_iota(jnp.int32, (experts, rows), 0)
    named = jnp.zeros((experts, rows), f32)
    for k in range(routes_t.shape[0]):
        named = named + (expert_row == routes_t[pl.ds(k, 1), :]).astype(f32)
    named = jnp.dot(placed, named.astype(bf16), preferred_element_type=f32)
    earlier = lax.broadcasted_iota(jnp.int32, (rows, rows), 0) < lax.broadcasted_iota(
        jnp.int32, (rows, rows), 1
    )
    before = jnp.dot(named.astype(bf16), earlier.astype(f32).astype(bf16), preferred_element_type=f32)
    slot = jnp.where(named > 0.5, before + 1.0, 0.0)
    router_p = jnp.dot(placed, router_t[...], preferred_element_type=f32).astype(bf16)
    logits = lax.dot_general(
        router_p, normed, (((1,), (1,)), ((), ())), preferred_element_type=f32
    )
    picked = jnp.where(named > 0.5, jax.nn.sigmoid(logits), 0.0)
    gates = picked / jnp.sum(picked, axis=0, keepdims=True)
    for zz in range(NZ):
        met[z, zz, pl.ds(0, NX), :] = slot[zz * NX : (zz + 1) * NX]
        met[z, zz, pl.ds(NX, NX), :] = gates[zz * NX : (zz + 1) * NX]

    piece = rows // PIECES
    last = NZ - 1
    behind_up = jnp.maximum(0, ((2 * z - last) * HOP + 3) // 4)
    behind_down = jnp.maximum(0, ((last - 2 * z) * HOP + 3) // 4)

    def piece_at(p):
        return pl.ds(pl.multiple_of(p * piece, piece), piece)

    def piece_to(way, s, p, zz):
        part_of = tok.at[s, piece_at(p)]
        return remote(part_of, part_of, ag_s.at[way, s, p], ag_r.at[s, p], at_z(zz))

    def table_to(way, s, zz):
        return remote(met.at[s], met.at[s], mg_s.at[way, s], mg_r.at[s], at_z(zz))

    def relay(way, k):
        t, p = k // PIECES, k % PIECES
        s = t if way == 0 else last - t
        inside = jnp.logical_and(k >= 0, t < NZ)
        comes = jnp.logical_and(inside, s < z if way == 0 else s > z)
        goes = jnp.logical_and(s <= z, z < last) if way == 0 else jnp.logical_and(s >= z, z > 0)
        goes = jnp.logical_and(inside, goes)
        to = jnp.minimum(z + 1, last) if way == 0 else jnp.maximum(z - 1, 0)

        @pl.when(jnp.logical_and(comes, p == 0))
        def _():
            table_to(way, s, to).wait_recv()

        @pl.when(jnp.logical_and(goes, p == 0))
        def _():
            table_to(way, s, to).start()

        @pl.when(comes)
        def _():
            piece_to(way, s, p, to).wait_recv()

        @pl.when(goes)
        def _():
            piece_to(way, s, p, to).start()

    def pair_at(tick, way):
        k = tick - jnp.where(way == 0, behind_up, behind_down)
        t = k // PIECES
        whole = jnp.logical_and(jnp.logical_and(k >= 0, t < NZ), k % PIECES == PIECES - 1)
        s = jnp.where(way == 0, t, last - t)
        odd = t % 2 == 1
        passed = jnp.logical_and(odd, jnp.where(way == 0, s < z, s > z))
        own_t = jnp.maximum(1, jnp.where(way == 0, z - 1, last - 1 - z))
        own = jnp.logical_and(z % 2 == 1 - way, t == own_t)
        valid = jnp.logical_and(whole, jnp.logical_or(passed, own))
        return jnp.where(valid, jnp.where(own, z // 2, s // 2), 0), valid

    def spread(q, row):
        pieces = []
        token_block = lax.broadcasted_iota(jnp.int32, (1, 2 * rows), 1) // rows
        for xx in range(NX):
            both = jnp.concatenate(
                [met[2 * q, z, pl.ds(row + xx, 1), :], met[2 * q + 1, z, pl.ds(row + xx, 1), :]], axis=1
            )
            for h in range(2):
                pieces.append(jnp.where(token_block == h, both, 0.0))
        return pieces

    slot_of = lax.broadcasted_iota(jnp.int32, (CAP, 2 * rows), 0).astype(f32) + 1.0
    pair_rows = 2 * CAP

    def gather(q):
        pick = jnp.concatenate([(line == slot_of).astype(f32) for line in spread(q, 0)], axis=0).astype(bf16)

        @pl.loop(0, width // 256)
        def _(n):
            cols = pl.ds(pl.multiple_of(n * 256, 256), 256)
            pair = tok[pl.ds(2 * q, 2), :, cols].reshape(2 * rows, 256)
            got = jnp.dot(pick, pair, preferred_element_type=f32).astype(bf16)
            for xx in range(NX):
                xs[q, xx, :, cols] = got[xx * pair_rows : (xx + 1) * pair_rows]

        for j in range(1, NX):
            to = (x + j) % NX
            remote(xs.at[q, to], xr.at[q, x], xd_s.at[q, j], xd_r.at[q, j], at_x(to)).start()
        xr[q, x] = xs[q, x]

    def expert(q):
        for j in range(1, NX):
            src = (x + NX - j) % NX
            remote(xs.at[q, src], xr.at[q, src], xd_s.at[q, j], xd_r.at[q, j], at_x(src)).wait_recv()
        row_in = xr[q].reshape(NX * pair_rows, width)

        @pl.loop(0, ff // 256)
        def _(n):
            at_gate = pl.ds(pl.multiple_of(n * 256, 256), 256)
            at_up = pl.ds(pl.multiple_of(ff + n * 256, 256), 256)
            gate = jnp.dot(row_in, wgu[:, at_gate], preferred_element_type=f32)
            upper = jnp.dot(row_in, wgu[:, at_up], preferred_element_type=f32)
            hid[:, at_gate] = (jnp.maximum(gate, 0.0) * upper).astype(bf16)

        hidden = hid[...]

        @pl.loop(0, width // 256)
        def _(n):
            cols = pl.ds(pl.multiple_of(n * 256, 256), 256)
            got = jnp.dot(hidden, wdn[:, cols], preferred_element_type=f32).astype(bf16)
            for xx in range(NX):
                ys[q, xx, :, cols] = got[xx * pair_rows : (xx + 1) * pair_rows]

        for j in range(1, NX):
            to = (x + j) % NX
            remote(ys.at[q, to], yr.at[q, x], xb_s.at[q, j], xb_r.at[q, j], at_x(to)).start()
        yr[q, x] = ys[q, x]

    def mix(q):
        for j in range(1, NX):
            src = (x + NX - j) % NX
            remote(ys.at[q, src], yr.at[q, src], xb_s.at[q, j], xb_r.at[q, j], at_x(src)).wait_recv()
        weigh = jnp.concatenate(
            [
                jnp.where(line == slot_of, gate, 0.0)
                for line, gate in zip(spread(q, 0), spread(q, NX))
            ],
            axis=0,
        )
        high = weigh.astype(bf16)
        low = (weigh - high.astype(f32)).astype(bf16)
        high, low = high.T, low.T

        @pl.loop(0, width // 256)
        def _(n):
            cols = pl.ds(pl.multiple_of(n * 256, 256), 256)
            back = yr[q, :, :, cols].reshape(NX * pair_rows, 256)
            total = jnp.dot(high, back, preferred_element_type=f32) + jnp.dot(
                low, back, preferred_element_type=f32
            )
            part[pl.ds(2 * q, 2), :, cols] = total.reshape(2, rows, 256)

    def add_and_send(way, k):
        r, p = k // PIECES, k % PIECES
        s = r if way == 0 else last - r
        inside = jnp.logical_and(k >= 0, r < NZ)
        rin, rs_r = (rin_b, rs_rb) if way == 0 else (rin_f, rs_rf)
        first = z == (last if way == 0 else 0)
        to = jnp.maximum(z - 1, 0) if way == 0 else jnp.minimum(z + 1, last)

        @pl.when(jnp.logical_and(inside, s < z if way == 0 else s > z))
        def _():
            at = piece_at(p)
            copy = remote(rout.at[s, at], rin.at[s, at], rs_s.at[s, p], rs_r.at[s, p], at_z(to))

            @pl.when(first)
            def _():
                rout[s, at] = part[s, at].astype(bf16)

            @pl.when(jnp.logical_not(first))
            def _():
                copy.wait_recv()
                rout[s, at] = (part[s, at] + rin[s, at].astype(f32)).astype(bf16)

            copy.start()

    def stage(work, tick):
        def one(way, carry):
            q, valid = pair_at(tick, way)

            @pl.when(valid)
            def _():
                work(q)

            return carry

        lax.fori_loop(0, 2, one, 0)

    sum_down_at = behind_up + LAG_SUM + ((last - z) * 2 * HOP + 3) // 4
    sum_up_at = behind_down + LAG_SUM + (z * 2 * HOP + 3) // 4

    def step(tick, carry):
        weights_at(tick)
        relay(0, tick - behind_up)
        relay(1, tick - behind_down)
        stage(gather, tick)
        stage(expert, tick - LAG_EXPERT)
        stage(mix, tick - LAG_MIX)
        add_and_send(0, tick - sum_down_at)
        add_and_send(1, tick - sum_up_at)
        return carry

    lax.fori_loop(0, TICKS, step, 0)

    for p in range(PIECES):
        at = pl.ds(p * piece, piece)

        @pl.when(z < NZ - 1)
        def _():
            remote(rout.at[z, at], rin_b.at[z, at], rs_s.at[z, p], rs_rb.at[z, p], at_z(z + 1)).wait_recv()
            part[z, at] = part[z, at] + rin_b[z, at].astype(f32)

        @pl.when(z > 0)
        def _():
            remote(rout.at[z, at], rin_f.at[z, at], rs_s.at[z, p], rs_rf.at[z, p], at_z(z - 1)).wait_recv()
            part[z, at] = part[z, at] + rin_f[z, at].astype(f32)

        out[at, :] = part[z, at].astype(bf16)

    for p in parts:
        mate_out[p].wait_send()
        for j in range(NY):
            if j:
                own_out[j][p].wait_send()
                pass_out[j][p].wait_send()
            own_core[j][p].wait_send()
            mate_core[j][p].wait_send()

    def drain(s, carry):
        @pl.when(jnp.logical_and(s <= z, z < NZ - 1))
        def _():
            table_to(0, s, z + 1).wait_send()
            for p in range(PIECES):
                piece_to(0, s, p, z + 1).wait_send()

        @pl.when(jnp.logical_and(s >= z, z > 0))
        def _():
            table_to(1, s, z - 1).wait_send()
            for p in range(PIECES):
                piece_to(1, s, p, z - 1).wait_send()

        return carry

    lax.fori_loop(0, NZ, drain, 0)

    def drain_pair(q, carry):
        for j in range(1, NX):
            to = (x + j) % NX
            remote(xs.at[q, to], xr.at[q, x], xd_s.at[q, j], xd_r.at[q, j], at_x(to)).wait_send()
            remote(ys.at[q, to], yr.at[q, x], xb_s.at[q, j], xb_r.at[q, j], at_x(to)).wait_send()
        return carry

    lax.fori_loop(0, NZ // 2, drain_pair, 0)

    def drain_sum(s, carry):
        @pl.when(s != z)
        def _():
            for p in range(PIECES):
                at = pl.ds(p * piece, piece)
                remote(
                    rout.at[s, at], rin_b.at[s, at], rs_s.at[s, p], rs_rb.at[s, p],
                    at_z(jnp.where(s < z, z - 1, z + 1)),
                ).wait_send()

        return carry

    lax.fori_loop(0, NZ, drain_sum, 0)


def on_device(
    tokens, norm_gain, router_weight, routes, placement, gate_weight, up_weight, down_weight
):
    rows, width = tokens.shape
    experts = router_weight.shape[1]
    ff = gate_weight.shape[2]
    grows, drows = gate_weight.shape[1], down_weight.shape[1]
    blks = lax.axis_size("blk")
    bf16, f32 = jnp.bfloat16, jnp.float32
    dma = pltpu.SemaphoreType.DMA
    vmem = pl.BlockSpec(memory_space=pltpu.VMEM)
    hbm = pl.BlockSpec(memory_space=pl.ANY)
    rows_of = (NZ // 2, NX, 2 * CAP, width)
    return pl.pallas_call(
        kernel,
        out_shape=jax.ShapeDtypeStruct((rows, width), bf16),
        in_specs=[vmem] * 5 + [hbm] * 3,
        out_specs=vmem,
        scratch_shapes=[
            pltpu.VMEM((NZ, rows, width), bf16),
            pltpu.VMEM((NZ, NZ, 2 * NX, rows), f32),
            pltpu.VMEM((blks * grows, 2 * ff), bf16),
            pltpu.VMEM((blks * drows, width), bf16),
            pltpu.VMEM(rows_of, bf16),
            pltpu.VMEM(rows_of, bf16),
            pltpu.VMEM(rows_of, bf16),
            pltpu.VMEM(rows_of, bf16),
            pltpu.VMEM((NX * 2 * CAP, ff), bf16),
            pltpu.VMEM((NZ, rows, width), f32),
            pltpu.VMEM((NZ, rows, width), bf16),
            pltpu.VMEM((NZ, rows, width), bf16),
            pltpu.VMEM((NZ, rows, width), bf16),
            dma((3,)),
            dma((3,)), dma((3,)),
            dma((NY, 3)), dma((NY, 3)), dma((NY, 3)), dma((NY, 3)),
            dma((NY, 3)), dma((NY, 3)), dma((NY, 3)), dma((NY, 3)),
            dma((2, NZ, PIECES)), dma((NZ, PIECES)),
            dma((2, NZ)), dma((NZ,)),
            dma((NZ // 2, NX)), dma((NZ // 2, NX)), dma((NZ // 2, NX)), dma((NZ // 2, NX)),
            dma((NZ, PIECES)), dma((NZ, PIECES)), dma((NZ, PIECES)),
        ],
        compiler_params=pltpu.CompilerParams(
            collective_id=0, has_side_effects=True, vmem_limit_bytes=60 * 1024 * 1024
        ),
    )(
        tokens,
        norm_gain.reshape(1, width),
        routes.T,
        router_weight.T,
        placement.reshape(1, experts),
        gate_weight[0],
        up_weight[0],
        down_weight[0],
    )


def solution(mesh):
    in_specs = (
        P(("ep", "blk"), None),
        P(),
        P(),
        P(("ep", "blk"), None),
        P(),
        P("ep", "blk", None),
        P("ep", "blk", None),
        P("ep", "blk", None),
    )
    out_specs = P(("ep", "blk"), None)
    return jax.shard_map(
        on_device, mesh=mesh, in_specs=in_specs, out_specs=out_specs, check_vma=False
    )
```

```python
import functools

import jax
import jax.numpy as jnp
from jax import lax
from jax.experimental import pallas as pl
from jax.experimental.pallas import tpu as pltpu
from jax.sharding import PartitionSpec as P

MESH = pl.DeviceIdType.MESH
NZ, NX, NY = 8, 4, 4
CAP = 24
PIECES = 4
LAG_EXPERT = 5
LAG_MIX = 10
MID_EXPERT = 2
MID_MIX = 3
HOP = 12
SLOTS = 32
TICKS = (NZ - 1) * PIECES + ((NZ - 1) * HOP + 3) // 4 + PIECES + LAG_MIX + 4
MATE_AT = (4, 6, 9)
MATE_START = (-1, -1, -1, -1, 0, 1, 2, 3, 4)
OWN_ROWS_AT = 5
MATE_ROWS_AT = (8, 10, 12)


def kernel(
    tokens, gain, routes_t, router_t, placement, gate_w, up_w, down_w, out,
    tok, met, named_by, router_p, wgu, wdn, xs, xr, ys, yr, hid, part, rin_b, rin_f, rout,
    loc_sem, z_s, z_r, yo_s, yo_r, yp_s, yp_r, co_s, co_r, cp_s, cp_r,
    ag_s, ag_r, mg_s, mg_r, xd_s, xd_r, xb_s, xb_r, rs_s, rs_rb, rs_rf,
):
    f32, bf16 = jnp.float32, jnp.bfloat16
    ep, blk = lax.axis_index("ep"), lax.axis_index("blk")
    z, x = ep // NX, ep % NX
    y, zh, c = blk // 4, (blk // 2) % 2, blk % 2
    width = tokens.shape[1]
    rows = tokens.shape[0]
    grows, drows = gate_w.shape[0], down_w.shape[0]
    ff = gate_w.shape[1]

    def blk_of(yy, zz, cc):
        return ((yy + NY) % NY) * 4 + zz * 2 + cc

    def at_z(zz):
        return {"ep": zz * NX + x, "blk": blk}

    def at_y(j):
        return {"ep": ep, "blk": blk_of(y + j, zh, c)}

    def at_x(xx):
        return {"ep": z * NX + xx, "blk": blk}

    mate = {"ep": ep, "blk": blk_of(y, 1 - zh, c)}
    core = {"ep": ep, "blk": blk_of(y, zh, 1 - c)}

    def remote(src, dst, s, r, dev):
        return pltpu.make_async_remote_copy(
            src_ref=src, dst_ref=dst, send_sem=s, recv_sem=r, device_id=dev, device_id_type=MESH
        )

    def gu_at(b):
        return wgu.at[pl.ds(pl.multiple_of(b * grows, grows), grows)]

    def dn_at(b):
        return wdn.at[pl.ds(pl.multiple_of(b * drows, drows), drows)]

    own = pl.ds(pl.multiple_of(blk * grows, grows), grows)
    local = [
        pltpu.make_async_copy(gate_w, wgu.at[own, pl.ds(0, ff)], loc_sem.at[0]),
        pltpu.make_async_copy(up_w, wgu.at[own, pl.ds(ff, ff)], loc_sem.at[1]),
        pltpu.make_async_copy(down_w, dn_at(blk), loc_sem.at[2]),
    ]
    for copy in local:
        copy.start()

    barrier = pltpu.get_barrier_semaphore()

    def greet(dev):
        pl.semaphore_signal(barrier, inc=1, device_id=dev, device_id_type=MESH)

    greet(mate)
    greet(core)
    for j in range(1, NY):
        greet(at_y(j))
    for j in range(1, NX):
        greet(at_x((x + j) % NX))

    @pl.when(z > 0)
    def _():
        greet(at_z(z - 1))

    @pl.when(z < NZ - 1)
    def _():
        greet(at_z(z + 1))

    peers = 8 + (z > 0).astype(jnp.int32) + (z < NZ - 1).astype(jnp.int32)
    pl.semaphore_wait(barrier, peers)

    for copy in local:
        copy.wait()

    half_g = grows // 2

    def part_at(b, p):
        if p == 2:
            return dn_at(b)
        return wgu.at[pl.ds(pl.multiple_of(b * grows + p * half_g, half_g), half_g)]

    def part_to(b, p, s, r, dev):
        return remote(part_at(b, p), part_at(b, p), s, r, dev)

    last = NZ - 1
    middle = jnp.minimum(z, last - z)
    behind_up = jnp.maximum(0, ((2 * z - last) * HOP + 3) // 4)
    behind_down = jnp.maximum(0, ((last - 2 * z) * HOP + 3) // 4)
    behind = jnp.maximum(behind_up, behind_down)

    parts = range(3)
    mate_blk = blk_of(y, 1 - zh, c)

    def third_at(b, p, i):
        if p == 2:
            return wdn.at[pl.ds(pl.multiple_of(b * drows + i * (drows // 3), drows // 3), drows // 3)]
        return wgu.at[pl.ds(pl.multiple_of(b * grows + p * half_g + i * (half_g // 3), half_g // 3), half_g // 3)]

    mate_out = [remote(third_at(blk, p, i), third_at(blk, p, i), z_s.at[p, i], z_r.at[p, i], mate) for p in parts for i in range(3)]
    mate_in = [
        [remote(third_at(mate_blk, p, i), third_at(mate_blk, p, i), z_s.at[p, i], z_r.at[p, i], mate) for i in range(3)]
        for p in parts
    ]

    def y_copies(zz, s, r, far):
        return [
            [
                part_to(blk_of(y - j, zz, c) if far else blk_of(y, zz, c), p, s.at[j, p], r.at[j, p], at_y(j))
                for p in parts
            ]
            for j in range(NY)
        ]

    def core_copies(zz, cc, s, r):
        return [
            [part_to(blk_of(y - j, zz, cc), p, s.at[j, p], r.at[j, p], core) for p in parts]
            for j in range(NY)
        ]

    own_out, own_in = y_copies(zh, yo_s, yo_r, False), y_copies(zh, yo_s, yo_r, True)
    pass_out, pass_in = y_copies(1 - zh, yp_s, yp_r, False), y_copies(1 - zh, yp_s, yp_r, True)
    own_core, own_of_core = core_copies(zh, c, co_s, co_r), core_copies(zh, 1 - c, co_s, co_r)
    mate_core, mate_of_core = core_copies(1 - zh, c, cp_s, cp_r), core_copies(1 - zh, 1 - c, cp_s, cp_r)

    for at, copy in zip(MATE_START, mate_out):
        if at < 0:
            copy.start()
    for p in parts:
        for j in (1, 3, 2):
            own_out[j][p].start()
        own_core[0][p].start()

    def weights_at(t):
        for at, copy in zip(MATE_START, mate_out):
            if at >= 0:
                @pl.when(t == at)
                def _():
                    copy.start()

        for p in parts:
            @pl.when(t == MATE_AT[p])
            def _():
                for copy in mate_in[p]:
                    copy.wait_recv()
                for j in (1, 3, 2):
                    pass_out[j][p].start()
                mate_core[0][p].start()

        @pl.when(t == OWN_ROWS_AT)
        def _():
            for p in parts:
                for j in (1, 3, 2):
                    own_in[j][p].wait_recv()
                    own_core[j][p].start()

        for p in parts:
            @pl.when(t == MATE_ROWS_AT[p])
            def _():
                for j in (1, 3, 2):
                    pass_in[j][p].wait_recv()
                    mate_core[j][p].start()

        @pl.when(t == behind + PIECES - 1 + LAG_EXPERT + MID_EXPERT * middle)
        def _():
            for copies in own_of_core + mate_of_core:
                for copy in copies:
                    copy.wait_recv()

    values = tokens[...].astype(f32)
    square = jnp.mean(values * values, axis=-1, keepdims=True)
    normed = (values * lax.rsqrt(square + 1e-06) * gain[...].astype(f32)).astype(bf16)
    tok[z] = normed
    experts = router_t.shape[0]
    holder = lax.broadcasted_iota(jnp.int32, (experts, experts), 0)
    placed = (holder == placement[...]).astype(f32).astype(bf16)
    router_p[...] = jnp.dot(placed, router_t[...], preferred_element_type=f32).astype(bf16)
    named_by[z] = routes_t[...]

    def tables(s):
        expert_row = lax.broadcasted_iota(jnp.int32, (experts, rows), 0)
        named = jnp.zeros((experts, rows), f32)
        for k in range(routes_t.shape[0]):
            named = named + (expert_row == named_by[s, pl.ds(k, 1), :]).astype(f32)
        mapping = (lax.broadcasted_iota(jnp.int32, (experts, experts), 0) == placement[...]).astype(f32).astype(bf16)
        named = jnp.dot(mapping, named.astype(bf16), preferred_element_type=f32)
        earlier = lax.broadcasted_iota(jnp.int32, (rows, rows), 0) < lax.broadcasted_iota(
            jnp.int32, (rows, rows), 1
        )
        before = jnp.dot(named.astype(bf16), earlier.astype(f32).astype(bf16), preferred_element_type=f32)
        logits = lax.dot_general(
            router_p[...], tok[s], (((1,), (1,)), ((), ())), preferred_element_type=f32
        )
        picked = jnp.where(named > 0.5, jax.nn.sigmoid(logits), 0.0)
        met[s, pl.ds(0, experts), :] = jnp.where(named > 0.5, before + 1.0, 0.0)
        met[s, pl.ds(experts, experts), :] = picked / jnp.sum(picked, axis=0, keepdims=True)

    tables(z)

    piece = rows // PIECES
    def piece_at(p):
        return pl.ds(pl.multiple_of(p * piece, piece), piece)

    def piece_to(way, s, p, zz):
        part_of = tok.at[s, piece_at(p)]
        return remote(part_of, part_of, ag_s.at[way, s, p], ag_r.at[s, p], at_z(zz))

    def table_to(way, s, zz):
        return remote(named_by.at[s], named_by.at[s], mg_s.at[way, s], mg_r.at[s], at_z(zz))

    def relay(way, k):
        t, p = k // PIECES, k % PIECES
        s = t if way == 0 else last - t
        inside = jnp.logical_and(k >= 0, t < NZ)
        comes = jnp.logical_and(inside, s < z if way == 0 else s > z)
        goes = jnp.logical_and(s <= z, z < last) if way == 0 else jnp.logical_and(s >= z, z > 0)
        goes = jnp.logical_and(inside, goes)
        to = jnp.minimum(z + 1, last) if way == 0 else jnp.maximum(z - 1, 0)

        @pl.when(jnp.logical_and(comes, p == 0))
        def _():
            table_to(way, s, to).wait_recv()

        @pl.when(jnp.logical_and(goes, p == 0))
        def _():
            table_to(way, s, to).start()

        @pl.when(comes)
        def _():
            piece_to(way, s, p, to).wait_recv()

        @pl.when(goes)
        def _():
            piece_to(way, s, p, to).start()

    slot_of = lax.broadcasted_iota(jnp.int32, (SLOTS, rows), 0).astype(f32) + 1.0
    filled = pl.ds(0, CAP)

    def lines(s, row):
        return [met[s, pl.ds(row + z * NX + xx, 1), :] for xx in range(NX)]

    def gather(q):
        pick = jnp.concatenate([(line == slot_of).astype(f32) for line in lines(q, 0)], axis=0).astype(bf16)

        @pl.loop(0, width // 256)
        def _(n):
            cols = pl.ds(pl.multiple_of(n * 256, 256), 256)
            got = jnp.dot(pick, tok[q, :, cols], preferred_element_type=f32).astype(bf16)
            for xx in range(NX):
                xs[q, xx, :, cols] = got[xx * SLOTS : (xx + 1) * SLOTS]

        for j in range(1, NX):
            to = (x + j) % NX
            remote(xs.at[q, to, filled], xr.at[q, x, filled], xd_s.at[q, j], xd_r.at[q, j], at_x(to)).start()
        xr[q, x, filled] = xs[q, x, filled]

    def expert(q):
        for j in range(1, NX):
            src = (x + NX - j) % NX
            remote(xs.at[q, src, filled], xr.at[q, src, filled], xd_s.at[q, j], xd_r.at[q, j], at_x(src)).wait_recv()
        row_in = xr[q].reshape(NX * SLOTS, width)

        @pl.loop(0, ff // 256)
        def _(n):
            at_gate = pl.ds(pl.multiple_of(n * 256, 256), 256)
            at_up = pl.ds(pl.multiple_of(ff + n * 256, 256), 256)
            gate = jnp.dot(row_in, wgu[:, at_gate], preferred_element_type=f32)
            upper = jnp.dot(row_in, wgu[:, at_up], preferred_element_type=f32)
            hid[:, at_gate] = (jnp.maximum(gate, 0.0) * upper).astype(bf16)

        hidden = hid[...]

        @pl.loop(0, width // 256)
        def _(n):
            cols = pl.ds(pl.multiple_of(n * 256, 256), 256)
            got = jnp.dot(hidden, wdn[:, cols], preferred_element_type=f32).astype(bf16)
            for xx in range(NX):
                ys[q, xx, :, cols] = got[xx * SLOTS : (xx + 1) * SLOTS]

        for j in range(1, NX):
            to = (x + j) % NX
            remote(ys.at[q, to, filled], yr.at[q, x, filled], xb_s.at[q, j], xb_r.at[q, j], at_x(to)).start()
        yr[q, x, filled] = ys[q, x, filled]

    def mix(q):
        for j in range(1, NX):
            src = (x + NX - j) % NX
            remote(ys.at[q, src, filled], yr.at[q, src, filled], xb_s.at[q, j], xb_r.at[q, j], at_x(src)).wait_recv()
        weigh = jnp.concatenate(
            [
                jnp.where(line == slot_of, gate, 0.0)
                for line, gate in zip(lines(q, 0), lines(q, experts))
            ],
            axis=0,
        )
        high = weigh.astype(bf16)
        low = (weigh - high.astype(f32)).astype(bf16)
        high, low = high.T, low.T

        @pl.loop(0, width // 256)
        def _(n):
            cols = pl.ds(pl.multiple_of(n * 256, 256), 256)
            back = yr[q, :, :, cols].reshape(NX * SLOTS, 256)
            total = jnp.dot(high, back, preferred_element_type=f32) + jnp.dot(
                low, back, preferred_element_type=f32
            )
            part[q, :, cols] = total

    def add_and_send(way, k):
        r, p = k // PIECES, k % PIECES
        s = r if way == 0 else last - r
        inside = jnp.logical_and(k >= 0, r < NZ)
        rin, rs_r = (rin_b, rs_rb) if way == 0 else (rin_f, rs_rf)
        first = z == (last if way == 0 else 0)
        to = jnp.maximum(z - 1, 0) if way == 0 else jnp.minimum(z + 1, last)

        @pl.when(jnp.logical_and(inside, s < z if way == 0 else s > z))
        def _():
            at = piece_at(p)
            copy = remote(rout.at[s, at], rin.at[s, at], rs_s.at[s, p], rs_r.at[s, p], at_z(to))

            @pl.when(first)
            def _():
                rout[s, at] = part[s, at].astype(bf16)

            @pl.when(jnp.logical_not(first))
            def _():
                copy.wait_recv()
                rout[s, at] = (part[s, at] + rin[s, at].astype(f32)).astype(bf16)

            copy.start()

    def stage(work, tick, up, down, with_own):
        def one(way, carry):
            k = tick - jnp.where(way == 0, up, down)
            s = jnp.where(way == 0, k // PIECES, last - k // PIECES)
            comes = jnp.where(way == 0, s < z, s > z)
            inside = jnp.logical_and(k >= 0, k < NZ * PIECES)
            valid = jnp.logical_and(jnp.logical_and(inside, comes), k % PIECES == PIECES - 1)
            valid = jnp.where(way == 2, k == PIECES - 1, valid)
            s = jnp.where(way == 2, z, jnp.where(valid, s, 0))

            @pl.when(valid)
            def _():
                work(s)

            return carry

        lax.fori_loop(0, 3 if with_own else 2, one, 0)

    sum_down_at = behind_up + PIECES - 1 + LAG_MIX + ((last - z) * 2 * HOP + 3) // 4
    sum_up_at = behind_down + PIECES - 1 + LAG_MIX + (z * 2 * HOP + 3) // 4

    for s in range(NZ):
        for xx in range(NX):
            empty = jnp.zeros((SLOTS - CAP, width), bf16)
            xr[s, xx, pl.ds(CAP, SLOTS - CAP)] = empty
            yr[s, xx, pl.ds(CAP, SLOTS - CAP)] = empty
    gather(z)

    def step(tick, carry):
        relay(0, tick - behind_up)
        relay(1, tick - behind_down)
        weights_at(tick)
        stage(tables, tick, behind_up, behind_down, False)
        stage(gather, tick, behind_up, behind_down, False)
        stage(expert, tick - LAG_EXPERT - MID_EXPERT * middle, behind, behind, True)
        stage(mix, tick - LAG_MIX - MID_MIX * middle, behind, behind, True)
        add_and_send(0, tick - sum_down_at)
        add_and_send(1, tick - sum_up_at)
        return carry

    lax.fori_loop(0, TICKS, step, 0)

    for p in range(PIECES):
        at = pl.ds(p * piece, piece)

        @pl.when(z < NZ - 1)
        def _():
            remote(rout.at[z, at], rin_b.at[z, at], rs_s.at[z, p], rs_rb.at[z, p], at_z(z + 1)).wait_recv()
            part[z, at] = part[z, at] + rin_b[z, at].astype(f32)

        @pl.when(z > 0)
        def _():
            remote(rout.at[z, at], rin_f.at[z, at], rs_s.at[z, p], rs_rf.at[z, p], at_z(z - 1)).wait_recv()
            part[z, at] = part[z, at] + rin_f[z, at].astype(f32)

        out[at, :] = part[z, at].astype(bf16)

    for p in parts:
        for copy in mate_in[p]:
            copy.wait_send()
        for j in range(NY):
            if j:
                own_out[j][p].wait_send()
                pass_out[j][p].wait_send()
            own_core[j][p].wait_send()
            mate_core[j][p].wait_send()

    def drain(s, carry):
        @pl.when(jnp.logical_and(s <= z, z < NZ - 1))
        def _():
            table_to(0, s, z + 1).wait_send()
            for p in range(PIECES):
                piece_to(0, s, p, z + 1).wait_send()

        @pl.when(jnp.logical_and(s >= z, z > 0))
        def _():
            table_to(1, s, z - 1).wait_send()
            for p in range(PIECES):
                piece_to(1, s, p, z - 1).wait_send()

        return carry

    lax.fori_loop(0, NZ, drain, 0)

    def drain_rows(q, carry):
        for j in range(1, NX):
            to = (x + j) % NX
            remote(xs.at[q, to, filled], xr.at[q, x, filled], xd_s.at[q, j], xd_r.at[q, j], at_x(to)).wait_send()
            remote(ys.at[q, to, filled], yr.at[q, x, filled], xb_s.at[q, j], xb_r.at[q, j], at_x(to)).wait_send()
        return carry

    lax.fori_loop(0, NZ, drain_rows, 0)

    def drain_sum(s, carry):
        @pl.when(s != z)
        def _():
            for p in range(PIECES):
                at = pl.ds(p * piece, piece)
                remote(
                    rout.at[s, at], rin_b.at[s, at], rs_s.at[s, p], rs_rb.at[s, p],
                    at_z(jnp.where(s < z, z - 1, z + 1)),
                ).wait_send()

        return carry

    lax.fori_loop(0, NZ, drain_sum, 0)


def on_device(
    tokens, norm_gain, router_weight, routes, placement, gate_weight, up_weight, down_weight
):
    rows, width = tokens.shape
    experts = router_weight.shape[1]
    ff = gate_weight.shape[2]
    grows, drows = gate_weight.shape[1], down_weight.shape[1]
    blks = lax.axis_size("blk")
    bf16, f32 = jnp.bfloat16, jnp.float32
    dma = pltpu.SemaphoreType.DMA
    vmem = pl.BlockSpec(memory_space=pltpu.VMEM)
    hbm = pl.BlockSpec(memory_space=pl.ANY)
    rows_of = (NZ, NX, SLOTS, width)
    return pl.pallas_call(
        kernel,
        out_shape=jax.ShapeDtypeStruct((rows, width), bf16),
        in_specs=[vmem] * 5 + [hbm] * 3,
        out_specs=vmem,
        scratch_shapes=[
            pltpu.VMEM((NZ, rows, width), bf16),
            pltpu.VMEM((NZ, 2 * experts, rows), f32),
            pltpu.VMEM((NZ, routes.shape[1], rows), jnp.int32),
            pltpu.VMEM((experts, width), bf16),
            pltpu.VMEM((blks * grows, 2 * ff), bf16),
            pltpu.VMEM((blks * drows, width), bf16),
            pltpu.VMEM(rows_of, bf16),
            pltpu.VMEM(rows_of, bf16),
            pltpu.VMEM(rows_of, bf16),
            pltpu.VMEM(rows_of, bf16),
            pltpu.VMEM((NX * SLOTS, ff), bf16),
            pltpu.VMEM((NZ, rows, width), f32),
            pltpu.VMEM((NZ, rows, width), bf16),
            pltpu.VMEM((NZ, rows, width), bf16),
            pltpu.VMEM((NZ, rows, width), bf16),
            dma((3,)),
            dma((3, 3)), dma((3, 3)),
            dma((NY, 3)), dma((NY, 3)), dma((NY, 3)), dma((NY, 3)),
            dma((NY, 3)), dma((NY, 3)), dma((NY, 3)), dma((NY, 3)),
            dma((2, NZ, PIECES)), dma((NZ, PIECES)),
            dma((2, NZ)), dma((NZ,)),
            dma((NZ, NX)), dma((NZ, NX)), dma((NZ, NX)), dma((NZ, NX)),
            dma((NZ, PIECES)), dma((NZ, PIECES)), dma((NZ, PIECES)),
        ],
        compiler_params=pltpu.CompilerParams(
            collective_id=0, has_side_effects=True, vmem_limit_bytes=60 * 1024 * 1024
        ),
    )(
        tokens,
        norm_gain.reshape(1, width),
        routes.T,
        router_weight.T,
        placement.reshape(1, experts),
        gate_weight[0],
        up_weight[0],
        down_weight[0],
    )


def solution(mesh):
    in_specs = (
        P(("ep", "blk"), None),
        P(),
        P(),
        P(("ep", "blk"), None),
        P(),
        P("ep", "blk", None),
        P("ep", "blk", None),
        P("ep", "blk", None),
    )
    out_specs = P(("ep", "blk"), None)
    return jax.shard_map(
        on_device, mesh=mesh, in_specs=in_specs, out_specs=out_specs, check_vma=False
    )
```

```python
import functools

import jax
import jax.numpy as jnp
from jax import lax
from jax.experimental import pallas as pl
from jax.experimental.pallas import tpu as pltpu
from jax.sharding import PartitionSpec as P

MESH = pl.DeviceIdType.MESH
NZ, NX, NY = 8, 4, 4
CAP = 24
PIECES = 4
LAG_EXPERT = 4
LAG_MIX = 8
MID_EXPERT = 2
MID_MIX = 3
HOP = 12
SLOTS = 32
TICKS = (NZ - 1) * PIECES + ((NZ - 1) * HOP + 3) // 4 + PIECES + LAG_MIX + 4
MATE_AT = (4, 6, 9)
MATE_START = (-1, -1, -1, -1, 0, 1, 2, 3, 4)
OWN_ROWS_AT = 5
MATE_ROWS_AT = (8, 10, 12)


def kernel(
    tokens, gain, routes_t, router_t, placement, gate_w, up_w, down_w, out,
    tok, met, named_by, router_p, wgu, wdn, xs, xr, ys, yr, hid, part, rin_b, rin_f, rout,
    loc_sem, z_s, z_r, yo_s, yo_r, yp_s, yp_r, co_s, co_r, cp_s, cp_r,
    ag_s, ag_r, mg_s, mg_r, xd_s, xd_r, xb_s, xb_r, rs_s, rs_rb, rs_rf,
):
    f32, bf16 = jnp.float32, jnp.bfloat16
    ep, blk = lax.axis_index("ep"), lax.axis_index("blk")
    z, x = ep // NX, ep % NX
    y, zh, c = blk // 4, (blk // 2) % 2, blk % 2
    width = tokens.shape[1]
    rows = tokens.shape[0]
    grows, drows = gate_w.shape[0], down_w.shape[0]
    ff = gate_w.shape[1]

    def blk_of(yy, zz, cc):
        return ((yy + NY) % NY) * 4 + zz * 2 + cc

    def at_z(zz):
        return {"ep": zz * NX + x, "blk": blk}

    def at_y(j):
        return {"ep": ep, "blk": blk_of(y + j, zh, c)}

    def at_x(xx):
        return {"ep": z * NX + xx, "blk": blk}

    mate = {"ep": ep, "blk": blk_of(y, 1 - zh, c)}
    core = {"ep": ep, "blk": blk_of(y, zh, 1 - c)}

    def remote(src, dst, s, r, dev):
        return pltpu.make_async_remote_copy(
            src_ref=src, dst_ref=dst, send_sem=s, recv_sem=r, device_id=dev, device_id_type=MESH
        )

    def gu_at(b):
        return wgu.at[pl.ds(pl.multiple_of(b * grows, grows), grows)]

    def dn_at(b):
        return wdn.at[pl.ds(pl.multiple_of(b * drows, drows), drows)]

    own = pl.ds(pl.multiple_of(blk * grows, grows), grows)
    local = [
        pltpu.make_async_copy(gate_w, wgu.at[own, pl.ds(0, ff)], loc_sem.at[0]),
        pltpu.make_async_copy(up_w, wgu.at[own, pl.ds(ff, ff)], loc_sem.at[1]),
        pltpu.make_async_copy(down_w, dn_at(blk), loc_sem.at[2]),
    ]
    for copy in local:
        copy.start()

    barrier = pltpu.get_barrier_semaphore()

    def greet(dev):
        pl.semaphore_signal(barrier, inc=1, device_id=dev, device_id_type=MESH)

    greet(mate)
    greet(core)
    for j in range(1, NY):
        greet(at_y(j))
    for j in range(1, NX):
        greet(at_x((x + j) % NX))

    @pl.when(z > 0)
    def _():
        greet(at_z(z - 1))

    @pl.when(z < NZ - 1)
    def _():
        greet(at_z(z + 1))

    peers = 8 + (z > 0).astype(jnp.int32) + (z < NZ - 1).astype(jnp.int32)
    pl.semaphore_wait(barrier, peers)

    for copy in local:
        copy.wait()

    half_g = grows // 2

    def part_at(b, p):
        if p == 2:
            return dn_at(b)
        return wgu.at[pl.ds(pl.multiple_of(b * grows + p * half_g, half_g), half_g)]

    def part_to(b, p, s, r, dev):
        return remote(part_at(b, p), part_at(b, p), s, r, dev)

    last = NZ - 1
    middle = jnp.minimum(z, last - z)
    behind_up = jnp.maximum(0, ((2 * z - last) * HOP + 3) // 4)
    behind_down = jnp.maximum(0, ((last - 2 * z) * HOP + 3) // 4)
    behind = jnp.maximum(behind_up, behind_down)

    parts = range(3)
    mate_blk = blk_of(y, 1 - zh, c)

    def third_at(b, p, i):
        if p == 2:
            return wdn.at[pl.ds(pl.multiple_of(b * drows + i * (drows // 3), drows // 3), drows // 3)]
        return wgu.at[pl.ds(pl.multiple_of(b * grows + p * half_g + i * (half_g // 3), half_g // 3), half_g // 3)]

    mate_out = [remote(third_at(blk, p, i), third_at(blk, p, i), z_s.at[p, i], z_r.at[p, i], mate) for p in parts for i in range(3)]
    mate_in = [
        [remote(third_at(mate_blk, p, i), third_at(mate_blk, p, i), z_s.at[p, i], z_r.at[p, i], mate) for i in range(3)]
        for p in parts
    ]

    def y_copies(zz, s, r, far):
        return [
            [
                part_to(blk_of(y - j, zz, c) if far else blk_of(y, zz, c), p, s.at[j, p], r.at[j, p], at_y(j))
                for p in parts
            ]
            for j in range(NY)
        ]

    def core_copies(zz, cc, s, r):
        return [
            [part_to(blk_of(y - j, zz, cc), p, s.at[j, p], r.at[j, p], core) for p in parts]
            for j in range(NY)
        ]

    own_out, own_in = y_copies(zh, yo_s, yo_r, False), y_copies(zh, yo_s, yo_r, True)
    pass_out, pass_in = y_copies(1 - zh, yp_s, yp_r, False), y_copies(1 - zh, yp_s, yp_r, True)
    own_core, own_of_core = core_copies(zh, c, co_s, co_r), core_copies(zh, 1 - c, co_s, co_r)
    mate_core, mate_of_core = core_copies(1 - zh, c, cp_s, cp_r), core_copies(1 - zh, 1 - c, cp_s, cp_r)

    for at, copy in zip(MATE_START, mate_out):
        if at < 0:
            copy.start()
    for p in parts:
        for j in (1, 3, 2):
            own_out[j][p].start()
        own_core[0][p].start()

    def weights_at(t):
        for at, copy in zip(MATE_START, mate_out):
            if at >= 0:
                @pl.when(t == at)
                def _():
                    copy.start()

        for p in parts:
            @pl.when(t == MATE_AT[p])
            def _():
                for copy in mate_in[p]:
                    copy.wait_recv()
                for j in (1, 3, 2):
                    pass_out[j][p].start()
                mate_core[0][p].start()

        @pl.when(t == OWN_ROWS_AT)
        def _():
            for p in parts:
                for j in (1, 3, 2):
                    own_in[j][p].wait_recv()
                    own_core[j][p].start()

        for p in parts:
            @pl.when(t == MATE_ROWS_AT[p])
            def _():
                for j in (1, 3, 2):
                    pass_in[j][p].wait_recv()
                    mate_core[j][p].start()

        @pl.when(t == behind + PIECES - 1 + LAG_EXPERT + MID_EXPERT * middle)
        def _():
            for copies in own_of_core + mate_of_core:
                for copy in copies:
                    copy.wait_recv()

    values = tokens[...].astype(f32)
    square = jnp.mean(values * values, axis=-1, keepdims=True)
    normed = (values * lax.rsqrt(square + 1e-06) * gain[...].astype(f32)).astype(bf16)
    tok[z] = normed
    experts = router_t.shape[0]
    holder = lax.broadcasted_iota(jnp.int32, (experts, experts), 0)
    placed = (holder == placement[...]).astype(f32).astype(bf16)
    router_p[...] = jnp.dot(placed, router_t[...], preferred_element_type=f32).astype(bf16)
    named_by[z] = routes_t[...]

    def tables(s):
        expert_row = lax.broadcasted_iota(jnp.int32, (experts, rows), 0)
        named = jnp.zeros((experts, rows), f32)
        for k in range(routes_t.shape[0]):
            named = named + (expert_row == named_by[s, pl.ds(k, 1), :]).astype(f32)
        mapping = (lax.broadcasted_iota(jnp.int32, (experts, experts), 0) == placement[...]).astype(f32).astype(bf16)
        named = jnp.dot(mapping, named.astype(bf16), preferred_element_type=f32)
        earlier = lax.broadcasted_iota(jnp.int32, (rows, rows), 0) < lax.broadcasted_iota(
            jnp.int32, (rows, rows), 1
        )
        before = jnp.dot(named.astype(bf16), earlier.astype(f32).astype(bf16), preferred_element_type=f32)
        logits = lax.dot_general(
            router_p[...], tok[s], (((1,), (1,)), ((), ())), preferred_element_type=f32
        )
        picked = jnp.where(named > 0.5, jax.nn.sigmoid(logits), 0.0)
        met[s, pl.ds(0, experts), :] = jnp.where(named > 0.5, before + 1.0, 0.0)
        met[s, pl.ds(experts, experts), :] = picked / jnp.sum(picked, axis=0, keepdims=True)

    tables(z)

    piece = rows // PIECES
    def piece_at(p):
        return pl.ds(pl.multiple_of(p * piece, piece), piece)

    def piece_to(way, s, p, zz):
        part_of = tok.at[s, piece_at(p)]
        return remote(part_of, part_of, ag_s.at[way, s, p], ag_r.at[s, p], at_z(zz))

    def table_to(way, s, zz):
        return remote(named_by.at[s], named_by.at[s], mg_s.at[way, s], mg_r.at[s], at_z(zz))

    def relay(way, k):
        t, p = k // PIECES, k % PIECES
        s = t if way == 0 else last - t
        inside = jnp.logical_and(k >= 0, t < NZ)
        comes = jnp.logical_and(inside, s < z if way == 0 else s > z)
        goes = jnp.logical_and(s <= z, z < last) if way == 0 else jnp.logical_and(s >= z, z > 0)
        goes = jnp.logical_and(inside, goes)
        to = jnp.minimum(z + 1, last) if way == 0 else jnp.maximum(z - 1, 0)

        @pl.when(jnp.logical_and(comes, p == 0))
        def _():
            table_to(way, s, to).wait_recv()

        @pl.when(jnp.logical_and(goes, p == 0))
        def _():
            table_to(way, s, to).start()

        @pl.when(comes)
        def _():
            piece_to(way, s, p, to).wait_recv()

        @pl.when(goes)
        def _():
            piece_to(way, s, p, to).start()

    slot_of = lax.broadcasted_iota(jnp.int32, (SLOTS, rows), 0).astype(f32) + 1.0
    filled = pl.ds(0, CAP)

    def lines(s, row):
        return [met[s, pl.ds(row + z * NX + xx, 1), :] for xx in range(NX)]

    def gather(q):
        pick = jnp.concatenate([(line == slot_of).astype(f32) for line in lines(q, 0)], axis=0).astype(bf16)

        @pl.loop(0, width // 256)
        def _(n):
            cols = pl.ds(pl.multiple_of(n * 256, 256), 256)
            got = jnp.dot(pick, tok[q, :, cols], preferred_element_type=f32).astype(bf16)
            for xx in range(NX):
                xs[q, xx, :, cols] = got[xx * SLOTS : (xx + 1) * SLOTS]

        for j in range(1, NX):
            to = (x + j) % NX
            remote(xs.at[q, to, filled], xr.at[q, x, filled], xd_s.at[q, j], xd_r.at[q, j], at_x(to)).start()
        xr[q, x, filled] = xs[q, x, filled]

    def expert(q):
        for j in range(1, NX):
            src = (x + NX - j) % NX
            remote(xs.at[q, src, filled], xr.at[q, src, filled], xd_s.at[q, j], xd_r.at[q, j], at_x(src)).wait_recv()
        row_in = xr[q].reshape(NX * SLOTS, width)

        @pl.loop(0, ff // 256)
        def _(n):
            at_gate = pl.ds(pl.multiple_of(n * 256, 256), 256)
            at_up = pl.ds(pl.multiple_of(ff + n * 256, 256), 256)
            gate = jnp.dot(row_in, wgu[:, at_gate], preferred_element_type=f32)
            upper = jnp.dot(row_in, wgu[:, at_up], preferred_element_type=f32)
            hid[:, at_gate] = (jnp.maximum(gate, 0.0) * upper).astype(bf16)

        hidden = hid[...]

        @pl.loop(0, width // 256)
        def _(n):
            cols = pl.ds(pl.multiple_of(n * 256, 256), 256)
            got = jnp.dot(hidden, wdn[:, cols], preferred_element_type=f32).astype(bf16)
            for xx in range(NX):
                ys[q, xx, :, cols] = got[xx * SLOTS : (xx + 1) * SLOTS]

        for j in range(1, NX):
            to = (x + j) % NX
            remote(ys.at[q, to, filled], yr.at[q, x, filled], xb_s.at[q, j], xb_r.at[q, j], at_x(to)).start()
        yr[q, x, filled] = ys[q, x, filled]

    def mix(q):
        for j in range(1, NX):
            src = (x + NX - j) % NX
            remote(ys.at[q, src, filled], yr.at[q, src, filled], xb_s.at[q, j], xb_r.at[q, j], at_x(src)).wait_recv()
        weigh = jnp.concatenate(
            [
                jnp.where(line == slot_of, gate, 0.0)
                for line, gate in zip(lines(q, 0), lines(q, experts))
            ],
            axis=0,
        )
        high = weigh.astype(bf16)
        low = (weigh - high.astype(f32)).astype(bf16)
        high, low = high.T, low.T

        @pl.loop(0, width // 256)
        def _(n):
            cols = pl.ds(pl.multiple_of(n * 256, 256), 256)
            back = yr[q, :, :, cols].reshape(NX * SLOTS, 256)
            total = jnp.dot(high, back, preferred_element_type=f32) + jnp.dot(
                low, back, preferred_element_type=f32
            )
            part[q, :, cols] = total

    def add_and_send(way, k):
        r, p = k // PIECES, k % PIECES
        s = r if way == 0 else last - r
        inside = jnp.logical_and(k >= 0, r < NZ)
        rin, rs_r = (rin_b, rs_rb) if way == 0 else (rin_f, rs_rf)
        first = z == (last if way == 0 else 0)
        to = jnp.maximum(z - 1, 0) if way == 0 else jnp.minimum(z + 1, last)

        @pl.when(jnp.logical_and(inside, s < z if way == 0 else s > z))
        def _():
            at = piece_at(p)
            copy = remote(rout.at[s, at], rin.at[s, at], rs_s.at[s, p], rs_r.at[s, p], at_z(to))

            @pl.when(first)
            def _():
                rout[s, at] = part[s, at].astype(bf16)

            @pl.when(jnp.logical_not(first))
            def _():
                copy.wait_recv()
                rout[s, at] = (part[s, at] + rin[s, at].astype(f32)).astype(bf16)

            copy.start()

    def stage(work, tick, up, down, with_own):
        def one(way, carry):
            k = tick - jnp.where(way == 0, up, down)
            s = jnp.where(way == 0, k // PIECES, last - k // PIECES)
            comes = jnp.where(way == 0, s < z, s > z)
            inside = jnp.logical_and(k >= 0, k < NZ * PIECES)
            valid = jnp.logical_and(jnp.logical_and(inside, comes), k % PIECES == PIECES - 1)
            valid = jnp.where(way == 2, k == PIECES - 1, valid)
            s = jnp.where(way == 2, z, jnp.where(valid, s, 0))

            @pl.when(valid)
            def _():
                work(s)

            return carry

        lax.fori_loop(0, 3 if with_own else 2, one, 0)

    sum_down_at = behind_up + PIECES - 1 + LAG_MIX + ((last - z) * 2 * HOP + 3) // 4
    sum_up_at = behind_down + PIECES - 1 + LAG_MIX + (z * 2 * HOP + 3) // 4

    for s in range(NZ):
        for xx in range(NX):
            empty = jnp.zeros((SLOTS - CAP, width), bf16)
            xr[s, xx, pl.ds(CAP, SLOTS - CAP)] = empty
            yr[s, xx, pl.ds(CAP, SLOTS - CAP)] = empty
    gather(z)

    def step(tick, carry):
        relay(0, tick - behind_up)
        relay(1, tick - behind_down)
        weights_at(tick)
        stage(tables, tick, behind_up, behind_down, False)
        stage(gather, tick, behind_up, behind_down, False)
        stage(expert, tick - LAG_EXPERT - MID_EXPERT * middle, behind, behind, True)
        stage(mix, tick - LAG_MIX - MID_MIX * middle, behind, behind, True)
        add_and_send(0, tick - sum_down_at)
        add_and_send(1, tick - sum_up_at)
        return carry

    lax.fori_loop(0, TICKS, step, 0)

    for p in range(PIECES):
        at = pl.ds(p * piece, piece)

        @pl.when(z < NZ - 1)
        def _():
            remote(rout.at[z, at], rin_b.at[z, at], rs_s.at[z, p], rs_rb.at[z, p], at_z(z + 1)).wait_recv()
            part[z, at] = part[z, at] + rin_b[z, at].astype(f32)

        @pl.when(z > 0)
        def _():
            remote(rout.at[z, at], rin_f.at[z, at], rs_s.at[z, p], rs_rf.at[z, p], at_z(z - 1)).wait_recv()
            part[z, at] = part[z, at] + rin_f[z, at].astype(f32)

        out[at, :] = part[z, at].astype(bf16)

    for p in parts:
        for copy in mate_in[p]:
            copy.wait_send()
        for j in range(NY):
            if j:
                own_out[j][p].wait_send()
                pass_out[j][p].wait_send()
            own_core[j][p].wait_send()
            mate_core[j][p].wait_send()

    def drain(s, carry):
        @pl.when(jnp.logical_and(s <= z, z < NZ - 1))
        def _():
            table_to(0, s, z + 1).wait_send()
            for p in range(PIECES):
                piece_to(0, s, p, z + 1).wait_send()

        @pl.when(jnp.logical_and(s >= z, z > 0))
        def _():
            table_to(1, s, z - 1).wait_send()
            for p in range(PIECES):
                piece_to(1, s, p, z - 1).wait_send()

        return carry

    lax.fori_loop(0, NZ, drain, 0)

    def drain_rows(q, carry):
        for j in range(1, NX):
            to = (x + j) % NX
            remote(xs.at[q, to, filled], xr.at[q, x, filled], xd_s.at[q, j], xd_r.at[q, j], at_x(to)).wait_send()
            remote(ys.at[q, to, filled], yr.at[q, x, filled], xb_s.at[q, j], xb_r.at[q, j], at_x(to)).wait_send()
        return carry

    lax.fori_loop(0, NZ, drain_rows, 0)

    def drain_sum(s, carry):
        @pl.when(s != z)
        def _():
            for p in range(PIECES):
                at = pl.ds(p * piece, piece)
                remote(
                    rout.at[s, at], rin_b.at[s, at], rs_s.at[s, p], rs_rb.at[s, p],
                    at_z(jnp.where(s < z, z - 1, z + 1)),
                ).wait_send()

        return carry

    lax.fori_loop(0, NZ, drain_sum, 0)


def on_device(
    tokens, norm_gain, router_weight, routes, placement, gate_weight, up_weight, down_weight
):
    rows, width = tokens.shape
    experts = router_weight.shape[1]
    ff = gate_weight.shape[2]
    grows, drows = gate_weight.shape[1], down_weight.shape[1]
    blks = lax.axis_size("blk")
    bf16, f32 = jnp.bfloat16, jnp.float32
    dma = pltpu.SemaphoreType.DMA
    vmem = pl.BlockSpec(memory_space=pltpu.VMEM)
    hbm = pl.BlockSpec(memory_space=pl.ANY)
    rows_of = (NZ, NX, SLOTS, width)
    return pl.pallas_call(
        kernel,
        out_shape=jax.ShapeDtypeStruct((rows, width), bf16),
        in_specs=[vmem] * 5 + [hbm] * 3,
        out_specs=vmem,
        scratch_shapes=[
            pltpu.VMEM((NZ, rows, width), bf16),
            pltpu.VMEM((NZ, 2 * experts, rows), f32),
            pltpu.VMEM((NZ, routes.shape[1], rows), jnp.int32),
            pltpu.VMEM((experts, width), bf16),
            pltpu.VMEM((blks * grows, 2 * ff), bf16),
            pltpu.VMEM((blks * drows, width), bf16),
            pltpu.VMEM(rows_of, bf16),
            pltpu.VMEM(rows_of, bf16),
            pltpu.VMEM(rows_of, bf16),
            pltpu.VMEM(rows_of, bf16),
            pltpu.VMEM((NX * SLOTS, ff), bf16),
            pltpu.VMEM((NZ, rows, width), f32),
            pltpu.VMEM((NZ, rows, width), bf16),
            pltpu.VMEM((NZ, rows, width), bf16),
            pltpu.VMEM((NZ, rows, width), bf16),
            dma((3,)),
            dma((3, 3)), dma((3, 3)),
            dma((NY, 3)), dma((NY, 3)), dma((NY, 3)), dma((NY, 3)),
            dma((NY, 3)), dma((NY, 3)), dma((NY, 3)), dma((NY, 3)),
            dma((2, NZ, PIECES)), dma((NZ, PIECES)),
            dma((2, NZ)), dma((NZ,)),
            dma((NZ, NX)), dma((NZ, NX)), dma((NZ, NX)), dma((NZ, NX)),
            dma((NZ, PIECES)), dma((NZ, PIECES)), dma((NZ, PIECES)),
        ],
        compiler_params=pltpu.CompilerParams(
            collective_id=0, has_side_effects=True, vmem_limit_bytes=60 * 1024 * 1024
        ),
    )(
        tokens,
        norm_gain.reshape(1, width),
        routes.T,
        router_weight.T,
        placement.reshape(1, experts),
        gate_weight[0],
        up_weight[0],
        down_weight[0],
    )


def solution(mesh):
    in_specs = (
        P(("ep", "blk"), None),
        P(),
        P(),
        P(("ep", "blk"), None),
        P(),
        P("ep", "blk", None),
        P("ep", "blk", None),
        P("ep", "blk", None),
    )
    out_specs = P(("ep", "blk"), None)
    return jax.shard_map(
        on_device, mesh=mesh, in_specs=in_specs, out_specs=out_specs, check_vma=False
    )
```

```python
import functools

import jax
import jax.numpy as jnp
from jax import lax
from jax.experimental import pallas as pl
from jax.experimental.pallas import tpu as pltpu
from jax.sharding import PartitionSpec as P

MESH = pl.DeviceIdType.MESH
NZ, NX, NY = 8, 4, 4
CAP = 24
PIECES = 4
LAG_EXPERT = 4
LAG_MIX = 8
MID_EXPERT = 2
MID_MIX = 3
HOP = 12
SLOTS = 32
TICKS = (NZ - 1) * PIECES + ((NZ - 1) * HOP + 3) // 4 + PIECES + LAG_MIX + 4
MATE_AT = (4, 7, 11)
MATE_START = (-1, -1, -1, -1, 0, 1, 2, 3, 4)
OWN_ROWS_AT = 5
MATE_ROWS_AT = (9, 12, 14)


def kernel(
    tokens, gain, routes_t, router_t, placement, gate_w, up_w, down_w, out,
    tok, met, named_by, router_p, wgu, wdn, xs, xr, ys, yr, hid, part, rin_b, rin_f, rout,
    loc_sem, z_s, z_r, yo_s, yo_r, yp_s, yp_r, co_s, co_r, cp_s, cp_r,
    ag_s, ag_r, mg_s, mg_r, xd_s, xd_r, xb_s, xb_r, rs_s, rs_rb, rs_rf,
):
    f32, bf16 = jnp.float32, jnp.bfloat16
    ep, blk = lax.axis_index("ep"), lax.axis_index("blk")
    z, x = ep // NX, ep % NX
    y, zh, c = blk // 4, (blk // 2) % 2, blk % 2
    width = tokens.shape[1]
    rows = tokens.shape[0]
    grows, drows = gate_w.shape[0], down_w.shape[0]
    ff = gate_w.shape[1]

    def blk_of(yy, zz, cc):
        return ((yy + NY) % NY) * 4 + zz * 2 + cc

    def at_z(zz):
        return {"ep": zz * NX + x, "blk": blk}

    def at_y(j):
        return {"ep": ep, "blk": blk_of(y + j, zh, c)}

    def at_x(xx):
        return {"ep": z * NX + xx, "blk": blk}

    mate = {"ep": ep, "blk": blk_of(y, 1 - zh, c)}
    core = {"ep": ep, "blk": blk_of(y, zh, 1 - c)}

    def remote(src, dst, s, r, dev):
        return pltpu.make_async_remote_copy(
            src_ref=src, dst_ref=dst, send_sem=s, recv_sem=r, device_id=dev, device_id_type=MESH
        )

    def gu_at(b):
        return wgu.at[pl.ds(pl.multiple_of(b * grows, grows), grows)]

    def dn_at(b):
        return wdn.at[pl.ds(pl.multiple_of(b * drows, drows), drows)]

    own = pl.ds(pl.multiple_of(blk * grows, grows), grows)
    local = [
        pltpu.make_async_copy(gate_w, wgu.at[own, pl.ds(0, ff)], loc_sem.at[0]),
        pltpu.make_async_copy(up_w, wgu.at[own, pl.ds(ff, ff)], loc_sem.at[1]),
        pltpu.make_async_copy(down_w, dn_at(blk), loc_sem.at[2]),
    ]
    for copy in local:
        copy.start()

    barrier = pltpu.get_barrier_semaphore()

    def greet(dev):
        pl.semaphore_signal(barrier, inc=1, device_id=dev, device_id_type=MESH)

    greet(mate)
    greet(core)
    for j in range(1, NY):
        greet(at_y(j))
    for j in range(1, NX):
        greet(at_x((x + j) % NX))

    @pl.when(z > 0)
    def _():
        greet(at_z(z - 1))

    @pl.when(z < NZ - 1)
    def _():
        greet(at_z(z + 1))

    peers = 8 + (z > 0).astype(jnp.int32) + (z < NZ - 1).astype(jnp.int32)
    pl.semaphore_wait(barrier, peers)

    for copy in local:
        copy.wait()

    half_g = grows // 2

    def part_at(b, p):
        if p == 2:
            return dn_at(b)
        return wgu.at[pl.ds(pl.multiple_of(b * grows + p * half_g, half_g), half_g)]

    def part_to(b, p, s, r, dev):
        return remote(part_at(b, p), part_at(b, p), s, r, dev)

    last = NZ - 1
    middle = jnp.minimum(z, last - z)
    behind_up = jnp.maximum(0, ((2 * z - last) * HOP + 3) // 4)
    behind_down = jnp.maximum(0, ((last - 2 * z) * HOP + 3) // 4)
    behind = jnp.maximum(behind_up, behind_down)

    parts = range(3)
    mate_blk = blk_of(y, 1 - zh, c)

    def third_at(b, p, i):
        if p == 2:
            return wdn.at[pl.ds(pl.multiple_of(b * drows + i * (drows // 3), drows // 3), drows // 3)]
        return wgu.at[pl.ds(pl.multiple_of(b * grows + p * half_g + i * (half_g // 3), half_g // 3), half_g // 3)]

    mate_out = [remote(third_at(blk, p, i), third_at(blk, p, i), z_s.at[p, i], z_r.at[p, i], mate) for p in parts for i in range(3)]
    mate_in = [
        [remote(third_at(mate_blk, p, i), third_at(mate_blk, p, i), z_s.at[p, i], z_r.at[p, i], mate) for i in range(3)]
        for p in parts
    ]

    def y_copies(zz, s, r, far):
        return [
            [
                part_to(blk_of(y - j, zz, c) if far else blk_of(y, zz, c), p, s.at[j, p], r.at[j, p], at_y(j))
                for p in parts
            ]
            for j in range(NY)
        ]

    def core_copies(zz, cc, s, r):
        return [
            [part_to(blk_of(y - j, zz, cc), p, s.at[j, p], r.at[j, p], core) for p in parts]
            for j in range(NY)
        ]

    own_out, own_in = y_copies(zh, yo_s, yo_r, False), y_copies(zh, yo_s, yo_r, True)
    pass_out, pass_in = y_copies(1 - zh, yp_s, yp_r, False), y_copies(1 - zh, yp_s, yp_r, True)
    own_core, own_of_core = core_copies(zh, c, co_s, co_r), core_copies(zh, 1 - c, co_s, co_r)
    mate_core, mate_of_core = core_copies(1 - zh, c, cp_s, cp_r), core_copies(1 - zh, 1 - c, cp_s, cp_r)

    for at, copy in zip(MATE_START, mate_out):
        if at < 0:
            copy.start()
    for p in parts:
        for j in (1, 3, 2):
            own_out[j][p].start()
        own_core[0][p].start()

    def weights_at(t):
        for at, copy in zip(MATE_START, mate_out):
            if at >= 0:
                @pl.when(t == at)
                def _():
                    copy.start()

        for p in parts:
            @pl.when(t == MATE_AT[p])
            def _():
                for copy in mate_in[p]:
                    copy.wait_recv()
                for j in (1, 3, 2):
                    pass_out[j][p].start()
                mate_core[0][p].start()

        @pl.when(t == OWN_ROWS_AT)
        def _():
            for p in parts:
                for j in (1, 3, 2):
                    own_in[j][p].wait_recv()
                    own_core[j][p].start()

        for p in parts:
            @pl.when(t == MATE_ROWS_AT[p])
            def _():
                for j in (1, 3, 2):
                    pass_in[j][p].wait_recv()
                    mate_core[j][p].start()

        @pl.when(t == behind + PIECES - 1 + LAG_EXPERT + MID_EXPERT * middle)
        def _():
            for copies in own_of_core + mate_of_core:
                for copy in copies:
                    copy.wait_recv()

    values = tokens[...].astype(f32)
    square = jnp.mean(values * values, axis=-1, keepdims=True)
    normed = (values * lax.rsqrt(square + 1e-06) * gain[...].astype(f32)).astype(bf16)
    tok[z] = normed
    experts = router_t.shape[0]
    holder = lax.broadcasted_iota(jnp.int32, (experts, experts), 0)
    placed = (holder == placement[...]).astype(f32).astype(bf16)
    router_p[...] = jnp.dot(placed, router_t[...], preferred_element_type=f32).astype(bf16)
    named_by[z] = routes_t[...]

    def tables(s):
        expert_row = lax.broadcasted_iota(jnp.int32, (experts, rows), 0)
        named = jnp.zeros((experts, rows), f32)
        for k in range(routes_t.shape[0]):
            named = named + (expert_row == named_by[s, pl.ds(k, 1), :]).astype(f32)
        mapping = (lax.broadcasted_iota(jnp.int32, (experts, experts), 0) == placement[...]).astype(f32).astype(bf16)
        named = jnp.dot(mapping, named.astype(bf16), preferred_element_type=f32)
        earlier = lax.broadcasted_iota(jnp.int32, (rows, rows), 0) < lax.broadcasted_iota(
            jnp.int32, (rows, rows), 1
        )
        before = jnp.dot(named.astype(bf16), earlier.astype(f32).astype(bf16), preferred_element_type=f32)
        logits = lax.dot_general(
            router_p[...], tok[s], (((1,), (1,)), ((), ())), preferred_element_type=f32
        )
        picked = jnp.where(named > 0.5, jax.nn.sigmoid(logits), 0.0)
        met[s, pl.ds(0, experts), :] = jnp.where(named > 0.5, before + 1.0, 0.0)
        met[s, pl.ds(experts, experts), :] = picked / jnp.sum(picked, axis=0, keepdims=True)

    tables(z)

    piece = rows // PIECES
    def piece_at(p):
        return pl.ds(pl.multiple_of(p * piece, piece), piece)

    def piece_to(way, s, p, zz):
        part_of = tok.at[s, piece_at(p)]
        return remote(part_of, part_of, ag_s.at[way, s, p], ag_r.at[s, p], at_z(zz))

    def table_to(way, s, zz):
        return remote(named_by.at[s], named_by.at[s], mg_s.at[way, s], mg_r.at[s], at_z(zz))

    def relay(way, k):
        t, p = k // PIECES, k % PIECES
        s = t if way == 0 else last - t
        inside = jnp.logical_and(k >= 0, t < NZ)
        comes = jnp.logical_and(inside, s < z if way == 0 else s > z)
        goes = jnp.logical_and(s <= z, z < last) if way == 0 else jnp.logical_and(s >= z, z > 0)
        goes = jnp.logical_and(inside, goes)
        to = jnp.minimum(z + 1, last) if way == 0 else jnp.maximum(z - 1, 0)

        @pl.when(jnp.logical_and(comes, p == 0))
        def _():
            table_to(way, s, to).wait_recv()

        @pl.when(jnp.logical_and(goes, p == 0))
        def _():
            table_to(way, s, to).start()

        @pl.when(comes)
        def _():
            piece_to(way, s, p, to).wait_recv()

        @pl.when(goes)
        def _():
            piece_to(way, s, p, to).start()

    slot_of = lax.broadcasted_iota(jnp.int32, (SLOTS, rows), 0).astype(f32) + 1.0
    filled = pl.ds(0, CAP)

    def lines(s, row):
        return [met[s, pl.ds(row + z * NX + xx, 1), :] for xx in range(NX)]

    def gather(q):
        pick = jnp.concatenate([(line == slot_of).astype(f32) for line in lines(q, 0)], axis=0).astype(bf16)

        @pl.loop(0, width // 256)
        def _(n):
            cols = pl.ds(pl.multiple_of(n * 256, 256), 256)
            got = jnp.dot(pick, tok[q, :, cols], preferred_element_type=f32).astype(bf16)
            for xx in range(NX):
                xs[q, xx, :, cols] = got[xx * SLOTS : (xx + 1) * SLOTS]

        for j in range(1, NX):
            to = (x + j) % NX
            remote(xs.at[q, to, filled], xr.at[q, x, filled], xd_s.at[q, j], xd_r.at[q, j], at_x(to)).start()
        xr[q, x, filled] = xs[q, x, filled]

    def expert(q):
        for j in range(1, NX):
            src = (x + NX - j) % NX
            remote(xs.at[q, src, filled], xr.at[q, src, filled], xd_s.at[q, j], xd_r.at[q, j], at_x(src)).wait_recv()
        row_in = xr[q].reshape(NX * SLOTS, width)

        @pl.loop(0, ff // 256)
        def _(n):
            at_gate = pl.ds(pl.multiple_of(n * 256, 256), 256)
            at_up = pl.ds(pl.multiple_of(ff + n * 256, 256), 256)
            gate = jnp.dot(row_in, wgu[:, at_gate], preferred_element_type=f32)
            upper = jnp.dot(row_in, wgu[:, at_up], preferred_element_type=f32)
            hid[:, at_gate] = (jnp.maximum(gate, 0.0) * upper).astype(bf16)

        hidden = hid[...]

        @pl.loop(0, width // 256)
        def _(n):
            cols = pl.ds(pl.multiple_of(n * 256, 256), 256)
            got = jnp.dot(hidden, wdn[:, cols], preferred_element_type=f32).astype(bf16)
            for xx in range(NX):
                ys[q, xx, :, cols] = got[xx * SLOTS : (xx + 1) * SLOTS]

        for j in range(1, NX):
            to = (x + j) % NX
            remote(ys.at[q, to, filled], yr.at[q, x, filled], xb_s.at[q, j], xb_r.at[q, j], at_x(to)).start()
        yr[q, x, filled] = ys[q, x, filled]

    def mix(q):
        for j in range(1, NX):
            src = (x + NX - j) % NX
            remote(ys.at[q, src, filled], yr.at[q, src, filled], xb_s.at[q, j], xb_r.at[q, j], at_x(src)).wait_recv()
        weigh = jnp.concatenate(
            [
                jnp.where(line == slot_of, gate, 0.0)
                for line, gate in zip(lines(q, 0), lines(q, experts))
            ],
            axis=0,
        )
        high = weigh.astype(bf16)
        low = (weigh - high.astype(f32)).astype(bf16)
        high, low = high.T, low.T

        @pl.loop(0, width // 256)
        def _(n):
            cols = pl.ds(pl.multiple_of(n * 256, 256), 256)
            back = yr[q, :, :, cols].reshape(NX * SLOTS, 256)
            total = jnp.dot(high, back, preferred_element_type=f32) + jnp.dot(
                low, back, preferred_element_type=f32
            )
            part[q, :, cols] = total

    def add_and_send(way, k):
        r, p = k // PIECES, k % PIECES
        s = r if way == 0 else last - r
        inside = jnp.logical_and(k >= 0, r < NZ)
        rin, rs_r = (rin_b, rs_rb) if way == 0 else (rin_f, rs_rf)
        first = z == (last if way == 0 else 0)
        to = jnp.maximum(z - 1, 0) if way == 0 else jnp.minimum(z + 1, last)

        @pl.when(jnp.logical_and(inside, s < z if way == 0 else s > z))
        def _():
            at = piece_at(p)
            copy = remote(rout.at[s, at], rin.at[s, at], rs_s.at[s, p], rs_r.at[s, p], at_z(to))

            @pl.when(first)
            def _():
                rout[s, at] = part[s, at].astype(bf16)

            @pl.when(jnp.logical_not(first))
            def _():
                copy.wait_recv()
                rout[s, at] = (part[s, at] + rin[s, at].astype(f32)).astype(bf16)

            copy.start()

    def stage(work, tick, up, down, with_own):
        def one(way, carry):
            k = tick - jnp.where(way == 0, up, down)
            s = jnp.where(way == 0, k // PIECES, last - k // PIECES)
            comes = jnp.where(way == 0, s < z, s > z)
            inside = jnp.logical_and(k >= 0, k < NZ * PIECES)
            valid = jnp.logical_and(jnp.logical_and(inside, comes), k % PIECES == PIECES - 1)
            valid = jnp.where(way == 2, k == PIECES - 1, valid)
            s = jnp.where(way == 2, z, jnp.where(valid, s, 0))

            @pl.when(valid)
            def _():
                work(s)

            return carry

        lax.fori_loop(0, 3 if with_own else 2, one, 0)

    sum_down_at = behind_up + PIECES - 1 + LAG_MIX + ((last - z) * 2 * HOP + 3) // 4
    sum_up_at = behind_down + PIECES - 1 + LAG_MIX + (z * 2 * HOP + 3) // 4

    for s in range(NZ):
        for xx in range(NX):
            empty = jnp.zeros((SLOTS - CAP, width), bf16)
            xr[s, xx, pl.ds(CAP, SLOTS - CAP)] = empty
            yr[s, xx, pl.ds(CAP, SLOTS - CAP)] = empty
    gather(z)

    def step(tick, carry):
        relay(0, tick - behind_up)
        relay(1, tick - behind_down)
        weights_at(tick)
        stage(tables, tick, behind_up, behind_down, False)
        stage(gather, tick, behind_up, behind_down, False)
        stage(expert, tick - LAG_EXPERT - MID_EXPERT * middle, behind, behind, True)
        stage(mix, tick - LAG_MIX - MID_MIX * middle, behind, behind, True)
        add_and_send(0, tick - sum_down_at)
        add_and_send(1, tick - sum_up_at)
        return carry

    lax.fori_loop(0, TICKS, step, 0)

    for p in range(PIECES):
        at = pl.ds(p * piece, piece)

        @pl.when(z < NZ - 1)
        def _():
            remote(rout.at[z, at], rin_b.at[z, at], rs_s.at[z, p], rs_rb.at[z, p], at_z(z + 1)).wait_recv()
            part[z, at] = part[z, at] + rin_b[z, at].astype(f32)

        @pl.when(z > 0)
        def _():
            remote(rout.at[z, at], rin_f.at[z, at], rs_s.at[z, p], rs_rf.at[z, p], at_z(z - 1)).wait_recv()
            part[z, at] = part[z, at] + rin_f[z, at].astype(f32)

        out[at, :] = part[z, at].astype(bf16)

    for p in parts:
        for copy in mate_in[p]:
            copy.wait_send()
        for j in range(NY):
            if j:
                own_out[j][p].wait_send()
                pass_out[j][p].wait_send()
            own_core[j][p].wait_send()
            mate_core[j][p].wait_send()

    def drain(s, carry):
        @pl.when(jnp.logical_and(s <= z, z < NZ - 1))
        def _():
            table_to(0, s, z + 1).wait_send()
            for p in range(PIECES):
                piece_to(0, s, p, z + 1).wait_send()

        @pl.when(jnp.logical_and(s >= z, z > 0))
        def _():
            table_to(1, s, z - 1).wait_send()
            for p in range(PIECES):
                piece_to(1, s, p, z - 1).wait_send()

        return carry

    lax.fori_loop(0, NZ, drain, 0)

    def drain_rows(q, carry):
        for j in range(1, NX):
            to = (x + j) % NX
            remote(xs.at[q, to, filled], xr.at[q, x, filled], xd_s.at[q, j], xd_r.at[q, j], at_x(to)).wait_send()
            remote(ys.at[q, to, filled], yr.at[q, x, filled], xb_s.at[q, j], xb_r.at[q, j], at_x(to)).wait_send()
        return carry

    lax.fori_loop(0, NZ, drain_rows, 0)

    def drain_sum(s, carry):
        @pl.when(s != z)
        def _():
            for p in range(PIECES):
                at = pl.ds(p * piece, piece)
                remote(
                    rout.at[s, at], rin_b.at[s, at], rs_s.at[s, p], rs_rb.at[s, p],
                    at_z(jnp.where(s < z, z - 1, z + 1)),
                ).wait_send()

        return carry

    lax.fori_loop(0, NZ, drain_sum, 0)


def on_device(
    tokens, norm_gain, router_weight, routes, placement, gate_weight, up_weight, down_weight
):
    rows, width = tokens.shape
    experts = router_weight.shape[1]
    ff = gate_weight.shape[2]
    grows, drows = gate_weight.shape[1], down_weight.shape[1]
    blks = lax.axis_size("blk")
    bf16, f32 = jnp.bfloat16, jnp.float32
    dma = pltpu.SemaphoreType.DMA
    vmem = pl.BlockSpec(memory_space=pltpu.VMEM)
    hbm = pl.BlockSpec(memory_space=pl.ANY)
    rows_of = (NZ, NX, SLOTS, width)
    return pl.pallas_call(
        kernel,
        out_shape=jax.ShapeDtypeStruct((rows, width), bf16),
        in_specs=[vmem] * 5 + [hbm] * 3,
        out_specs=vmem,
        scratch_shapes=[
            pltpu.VMEM((NZ, rows, width), bf16),
            pltpu.VMEM((NZ, 2 * experts, rows), f32),
            pltpu.VMEM((NZ, routes.shape[1], rows), jnp.int32),
            pltpu.VMEM((experts, width), bf16),
            pltpu.VMEM((blks * grows, 2 * ff), bf16),
            pltpu.VMEM((blks * drows, width), bf16),
            pltpu.VMEM(rows_of, bf16),
            pltpu.VMEM(rows_of, bf16),
            pltpu.VMEM(rows_of, bf16),
            pltpu.VMEM(rows_of, bf16),
            pltpu.VMEM((NX * SLOTS, ff), bf16),
            pltpu.VMEM((NZ, rows, width), f32),
            pltpu.VMEM((NZ, rows, width), bf16),
            pltpu.VMEM((NZ, rows, width), bf16),
            pltpu.VMEM((NZ, rows, width), bf16),
            dma((3,)),
            dma((3, 3)), dma((3, 3)),
            dma((NY, 3)), dma((NY, 3)), dma((NY, 3)), dma((NY, 3)),
            dma((NY, 3)), dma((NY, 3)), dma((NY, 3)), dma((NY, 3)),
            dma((2, NZ, PIECES)), dma((NZ, PIECES)),
            dma((2, NZ)), dma((NZ,)),
            dma((NZ, NX)), dma((NZ, NX)), dma((NZ, NX)), dma((NZ, NX)),
            dma((NZ, PIECES)), dma((NZ, PIECES)), dma((NZ, PIECES)),
        ],
        compiler_params=pltpu.CompilerParams(
            collective_id=0, has_side_effects=True, vmem_limit_bytes=60 * 1024 * 1024
        ),
    )(
        tokens,
        norm_gain.reshape(1, width),
        routes.T,
        router_weight.T,
        placement.reshape(1, experts),
        gate_weight[0],
        up_weight[0],
        down_weight[0],
    )


def solution(mesh):
    in_specs = (
        P(("ep", "blk"), None),
        P(),
        P(),
        P(("ep", "blk"), None),
        P(),
        P("ep", "blk", None),
        P("ep", "blk", None),
        P("ep", "blk", None),
    )
    out_specs = P(("ep", "blk"), None)
    return jax.shard_map(
        on_device, mesh=mesh, in_specs=in_specs, out_specs=out_specs, check_vma=False
    )
```
